256 devices in a mesh: seq: 8 (over z), tensor: 32 (over x, y, core).
Axes of the slice: x: 4, y: 4, z: 8, core: 2. Of those that a mesh axis runs over, the one named last changes fastest.
Arguments:
- tokens: bfloat16 [32768, 1536], P(('seq', 'tensor')), may hold values from -6 to 6
- segment_ids: int32 [32768], P(('seq', 'tensor')), may hold values from 0 to 31, never falling along the last dimension, each value on 1 to 4096 neighbouring positions
- page_table: int32 [8, 256], P('seq'), may hold values from 0 to 255, each once within a row
- attn_gain: float32 [1536], replicated, may hold values from 0.6 to 6
- w_qkv: bfloat16 [1536, 2048], P(None, 'tensor'), may hold values from -0.15625 to 0.15625
- w_out: bfloat16 [1536, 1536], P(None, 'tensor'), may hold values from -0.15625 to 0.15625
- moe_gain: float32 [1536], replicated, may hold values from 0.25 to 1.75
- route_ids: int32 [32768, 4], P(('seq', 'tensor')), may hold values from 0 to 31, all different within a row; in each aligned block of 128 rows (0 to 127, 128 to 255, ...) at most 24 rows name the same one
- route_weight: float32 [32768, 4], P(('seq', 'tensor')), may hold values from 0.05 to 1
- w_gate: bfloat16 [32, 1536, 768], P('tensor'), may hold values from -0.15625 to 0.15625
- w_up: bfloat16 [32, 1536, 768], P('tensor'), may hold values from -0.15625 to 0.15625
- w_down: bfloat16 [32, 768, 1536], P('tensor'), may hold values from -0.21875 to 0.21875
Outputs:
- mixed: bfloat16 [32768, 1536], P(('seq', 'tensor'))
- cache: bfloat16 [2048, 16, 512], P(('seq', 'tensor'))
The draws below stay inside these ranges and needn't reach their ends.
Inputs may be any that keep to these rules, and one draw needn't show every extreme that they name: `segment_ids`: segment numbers never fall along the tokens; every prompt spans 1 to 4096 tokens and one spans exactly 4096. `page_table`: each row is a permutation of the slots of one block. `route_ids`: each token names 4 different experts; among the rows of one device no expert is named more than 24 times, a bound that some block reaches.
All inputs are finite; a program needn't handle non-finite values.
Results may differ from the reference program's by a relative error of at most 0.012.
The reference program's roundings to bfloat16 on the way count: a program that leaves them out, or rounds other values in their place, can miss the bound.
Values may be sent and summed in bfloat16 or wider, within the bound.
A program may use at most 128 MiB of HBM per device.

```python
import math
import jax
import jax.numpy as jnp
import numpy as np
from jax import lax

D = 1536
HEADS = 12
KV_HEADS = 2
HEAD = 128
EXP_HID = 768
TOP = 4
PAGE = 16
TOK_DEV = 128
EXPERTS = 32
TOK_SEQ = 4096
TOKENS = 32768
SEG_MOST = 4096
SEGS = 32
CAP = 24
QKVW = 2048
PAGES_SEQ = 256
PAGES = 2048
N_SEQ = 8
N_TENSOR = 32


def draw_attn_gain(key, part):
    return jax.random.uniform(key, (D,), jnp.float32, 0.6, 1.6)


def block_scale(rng, shape, split, smallest, high):
    gain = 1.0
    for dim, shards_of in split:
        heights = jax.random.uniform(jax.random.fold_in(jax.random.fold_in(rng, 6), dim), (shards_of,), jnp.float32, smallest / len(split), high / len(split))
        gain = gain * jnp.repeat(jnp.exp(heights), shape[dim] // shards_of).reshape((-1,) + (1,) * (len(shape) - 1 - dim))
    return gain


def split_up(count, total, most, lean):
    loads = [(1 << 20) // math.isqrt(standing ** lean) + 1 for standing in range(2, count + 1)]
    rest, counts = total - most - (count - 1), [1] * (count - 1)
    while rest > 0:
        candidates = [i for i in range(count - 1) if counts[i] < most]
        pool, budget = sum([loads[i] for i in candidates]), rest
        for i in candidates:
            addition = min(most - counts[i], max(1, budget * loads[i] // pool), rest)
            counts[i] = counts[i] + addition
            rest = rest - addition
    return np.array([most] + counts)


def ragged(stream_key, number_of, total, limit, slope):
    if number_of == 2:
        one = jax.random.randint(stream_key, (), max(1, total - limit), min(limit, total - 1) + 1)
        return jnp.stack([one, total - one])
    sizes = jnp.asarray(split_up(number_of, total, limit, slope), jnp.int32)
    twos = (number_of - 1) // 2
    source_of, receiver = sizes[1:1 + 2 * twos:2], sizes[2:2 + 2 * twos:2]
    slack = jnp.minimum(source_of - 1, limit - receiver)
    passed = jax.random.randint(jax.random.fold_in(stream_key, 1), (twos,), 0, 1 << 20) % (slack + 1)
    sizes = sizes.at[1:1 + 2 * twos:2].set(source_of - passed).at[2:2 + 2 * twos:2].set(receiver + passed)
    return sizes[jax.random.permutation(jax.random.fold_in(stream_key, 2), number_of)]


def shared_out(stream_key, own, number, rows, count, top, limit, skew):
    sequence = jax.random.permutation(stream_key, count)
    heavy_load, common = portions_of(count, rows * top, limit, skew, True), portions_of(count, rows * top, limit, skew, False)
    places = jnp.arange(count)

    def named(sizes, offset_by):
        used = int((sizes > 0).sum())
        fixed = max(1, used // 4)
        passed = fixed + (places - fixed + offset_by * (used - fixed)) % max(1, count - fixed)
        return jnp.zeros((count,), jnp.int32).at[sequence[jnp.where(places < fixed, places, passed)]].set(jnp.asarray(sizes, jnp.int32))

    sizes = jnp.where(number % 4 == 0, named(heavy_load, number // 4), named(common, number - number // 4 - 1))
    mixed = jax.random.permutation(jax.random.fold_in(own, 3), count)
    giver, receiver = mixed[0:count // 2 * 2:2], mixed[1:count // 2 * 2:2]
    slack = jnp.minimum(sizes[giver] - 1, limit - sizes[receiver]) // 2
    slack = jnp.where((giver == sequence[0]) | (receiver == sequence[0]) | (sizes[receiver] == 0), 0, jnp.maximum(slack, 0))
    passed = jax.random.randint(jax.random.fold_in(own, 4), (count // 2,), 0, 1 << 20) % (slack + 1)
    sizes = sizes.at[giver].add(-passed).at[receiver].add(passed)
    items = jnp.searchsorted(jnp.cumsum(sizes), jnp.arange(rows * top), side="right").astype(jnp.int32)
    grid = items.reshape(top, rows).T
    grid = grid[jax.random.permutation(jax.random.fold_in(own, 1), rows)]
    offset_by = jax.random.randint(jax.random.fold_in(own, 2), (rows, 1), 0, top)
    return jnp.take_along_axis(grid, (jnp.arange(top)[None, :] + offset_by) % top, axis=1)


def portions_of(count, total, reach, skew, full):
    weights = [(1 << 20) // math.isqrt(rank ** skew) + 1 for rank in range(1, count + 1)]
    largest = reach if full else min(reach, max(-(-total // count), total * weights[0] // sum(weights)))
    least = 1 if total - largest >= count - 1 else 0
    holding, surplus = [largest] + [least] * (count - 1), total - largest - least * (count - 1)
    while surplus > 0:
        movable = [i for i in range(1, count) if holding[i] < largest] or [i for i in range(1, count) if holding[i] < reach]
        pool, remaining = sum([weights[i] for i in movable]), surplus
        for i in movable:
            addition = min(reach - holding[i], max(1, remaining * weights[i] // pool), surplus)
            holding[i] = holding[i] + addition
            surplus = surplus - addition
    return np.array(holding)


def gaussian(stream_key, shape, width, reach, shards=(), kind=jnp.bfloat16):
    factor_of = block_scale(stream_key, shape, shards, -0.22, 0.18) if shards else 1.0
    result = jax.random.normal(stream_key, shape, jnp.float32) * width * factor_of
    return jnp.minimum(jnp.maximum(result, -reach), reach).astype(kind)


def setup_inputs(seed: int = 0) -> dict:
    keys = jax.random.split(jax.random.key(seed), 13)
    tokens = gaussian(keys[0], (TOKENS, D), 1.0, 6.0, ((0, 256),))
    segment_ids = jnp.searchsorted(jnp.cumsum(ragged(keys[1], SEGS, TOKENS, SEG_MOST, 2)), jnp.arange(TOKENS), side="right").astype(jnp.int32)
    page_table = jax.vmap(lambda own: jax.random.permutation(own, PAGES_SEQ))(jax.random.split(keys[2], N_SEQ)).reshape((N_SEQ, PAGES_SEQ)).astype(jnp.int32)
    attn_gain = draw_attn_gain(jax.random.fold_in(keys[12], 71), 0)
    w_qkv = gaussian(keys[4], (D, QKVW), D ** -0.5, 0.15625, ((1, 32),))
    w_out = gaussian(keys[5], (HEADS * HEAD, D), (HEADS * HEAD) ** -0.5, 0.15625, ((1, 32),))
    moe_gain = jnp.clip(1.0 + 0.15 * jax.random.normal(keys[6], (D,), jnp.float32), 0.25, 1.75)
    route_ids_keys = jax.random.split(jax.random.fold_in(keys[7], 1), TOKENS // TOK_DEV)
    route_ids_turns = jax.random.permutation(jax.random.fold_in(keys[7], 3), TOKENS // TOK_DEV)
    route_ids = jax.vmap(lambda own, number: shared_out(jax.random.fold_in(keys[7], 2), own, number, TOK_DEV, EXPERTS, TOP, CAP, 2))(route_ids_keys, route_ids_turns).reshape((TOKENS, TOP))
    route_weight = jnp.clip(jnp.exp(math.log(1.0) - 2.9957323 * jax.random.uniform(keys[8], (TOKENS, TOP), jnp.float32) ** block_scale(keys[8], (TOKENS, TOP), ((0, 256),), -0.2, 0.2)), 0.05, 1.0)
    w_gate = gaussian(keys[9], (EXPERTS, D, EXP_HID), D ** -0.5, 0.15625, ((0, 32),))
    w_up = gaussian(keys[10], (EXPERTS, D, EXP_HID), D ** -0.5, 0.15625, ((0, 32),))
    w_down = gaussian(keys[11], (EXPERTS, EXP_HID, D), EXP_HID ** -0.5, 0.21875, ((0, 32),))
    return dict(tokens=tokens, segment_ids=segment_ids, page_table=page_table, attn_gain=attn_gain, w_qkv=w_qkv, w_out=w_out, moe_gain=moe_gain, route_ids=route_ids, route_weight=route_weight, w_gate=w_gate, w_up=w_up, w_down=w_down)


epsilon = 1e-06

def rms_scaled(values, scales):
    wide = values.astype(jnp.float32)
    mean_sq = lax.optimization_barrier(jnp.mean(wide * wide, axis=-1, keepdims=True))
    return (wide * lax.rsqrt(mean_sq + epsilon) * scales).astype(jnp.bfloat16)

def attend(queries, keys_window, values_window, allowed):
    scores = jnp.einsum('qhd,kd->hqk', queries.astype(jnp.float32), keys_window.astype(jnp.float32)) / math.sqrt(HEAD)
    scores = jnp.where(allowed[None], scores, -jnp.inf)
    highest = lax.optimization_barrier(jnp.max(scores, axis=-1, keepdims=True))
    weights = jnp.exp(scores - highest)
    totals = lax.optimization_barrier(jnp.sum(weights, axis=-1, keepdims=True))
    shares = (weights / totals).astype(jnp.bfloat16)
    return jnp.einsum('hqk,kd->qhd', shares.astype(jnp.float32), values_window.astype(jnp.float32))

def reference(tokens, segment_ids, page_table, attn_gain, w_qkv, w_out, moe_gain, route_ids, route_weight, w_gate, w_up, w_down):
    normed = rms_scaled(tokens, attn_gain)
    projected = jnp.dot(normed, w_qkv, preferred_element_type=jnp.float32).astype(jnp.bfloat16)
    query_width = HEADS * HEAD
    queries = projected[:, :query_width]
    all_kv = projected[:, query_width:]
    kv_width = all_kv.shape[1]
    pages = all_kv.reshape(N_SEQ, PAGES_SEQ, PAGE, kv_width)
    inverse = jnp.argsort(page_table, axis=1).astype(jnp.int32)
    cache = jnp.take_along_axis(pages, inverse[:, :, None, None], axis=1).reshape(PAGES, PAGE, kv_width)
    padded_kv = jnp.concatenate([jnp.zeros((TOK_SEQ, kv_width), jnp.bfloat16), all_kv], axis=0)
    padded_segs = jnp.concatenate([jnp.full((TOK_SEQ,), -1, jnp.int32), segment_ids], axis=0)
    window = TOK_SEQ + TOK_DEV
    per_group = HEADS // KV_HEADS

    def one_block(block_index):
        first_row = (block_index * TOK_DEV).astype(jnp.int32)
        keys_window = lax.dynamic_slice_in_dim(padded_kv, first_row, window, 0)
        segs_window = lax.dynamic_slice_in_dim(padded_segs, first_row, window, 0)
        query_rows = lax.dynamic_slice_in_dim(queries, first_row, TOK_DEV, 0).reshape(TOK_DEV, HEADS, HEAD)
        query_segs = lax.dynamic_slice_in_dim(segment_ids, first_row, TOK_DEV, 0)
        key_pos = first_row - TOK_SEQ + jnp.arange(window, dtype=jnp.int32)
        query_pos = first_row + jnp.arange(TOK_DEV, dtype=jnp.int32)
        allowed = (segs_window[None, :] == query_segs[:, None]) & (key_pos[None, :] <= query_pos[:, None])
        contexts = []
        for kv_group in range(KV_HEADS):
            key_cols = keys_window[:, kv_group * HEAD:(kv_group + 1) * HEAD]
            value_cols = keys_window[:, (KV_HEADS + kv_group) * HEAD:(KV_HEADS + kv_group + 1) * HEAD]
            contexts.append(attend(query_rows[:, kv_group * per_group:(kv_group + 1) * per_group], key_cols, value_cols, allowed))
        return jnp.concatenate(contexts, axis=1).reshape(TOK_DEV, query_width).astype(jnp.bfloat16)
    context = lax.map(one_block, jnp.arange(TOKENS // TOK_DEV, dtype=jnp.int32)).reshape(TOKENS, query_width)
    residual = (tokens.astype(jnp.float32) + jnp.dot(context, w_out, preferred_element_type=jnp.float32)).astype(jnp.bfloat16)
    expert_input = rms_scaled(residual, moe_gain)
    flat_routes = route_ids.reshape(-1)
    flat_weights = route_weight.reshape(-1)
    most_rows = N_SEQ * N_TENSOR * CAP

    def add_expert(running, expert_index):
        hits = flat_routes == expert_index
        counted = jnp.sum(hits.astype(jnp.int32))
        picked_pairs = jnp.nonzero(hits, size=most_rows, fill_value=0)[0].astype(jnp.int32)
        valid = jnp.arange(most_rows, dtype=jnp.int32) < counted
        pair_weights = jnp.where(valid, flat_weights[picked_pairs], jnp.zeros((), jnp.float32))
        token_rows = picked_pairs // TOP
        rows_in = expert_input[token_rows]
        gate_out = jnp.dot(rows_in, w_gate[expert_index], preferred_element_type=jnp.float32)
        up_out = jnp.dot(rows_in, w_up[expert_index], preferred_element_type=jnp.float32)
        hidden = (jnp.maximum(gate_out, 0.0) * up_out).astype(jnp.bfloat16)
        produced = jnp.dot(hidden, w_down[expert_index], preferred_element_type=jnp.float32).astype(jnp.bfloat16)
        return (running.at[token_rows].add(pair_weights[:, None] * produced.astype(jnp.float32)), None)
    summed = lax.scan(add_expert, jnp.zeros((TOKENS, D), jnp.float32), jnp.arange(EXPERTS, dtype=jnp.int32))[0]
    mixed = (residual.astype(jnp.float32) + summed).astype(jnp.bfloat16)
    return (mixed, cache)
```

```python
import functools
import math

import jax
import jax.numpy as jnp
from jax import lax
from jax.experimental import pallas as pl
from jax.experimental.pallas import tpu as pltpu
from jax.sharding import PartitionSpec as P

HEADS = 12
KV_HEADS = 2
HEAD = 128
TOP = 4
PAGE = 16
SEGS = 32
CHUNKS = 32
TOK = 128
STEP = 3
NEG = -1e30

epsilon = 1e-06
F32 = jnp.float32
BF16 = jnp.bfloat16


def rms_scaled(values, scales):
    wide = values.astype(F32)
    mean_sq = jnp.mean(wide * wide, axis=-1, keepdims=True)
    return (wide * lax.rsqrt(mean_sq + epsilon) * scales).astype(BF16)


def attention_kernel(starts_ref, q_ref, kv_ref, out_ref, top, total, acc):
    place = lax.axis_index("tensor")
    scale = math.log2(math.e) / math.sqrt(HEAD)
    group_heads = HEADS // KV_HEADS
    top[...] = jnp.full_like(top, NEG)
    total[...] = jnp.zeros_like(total)
    acc[...] = jnp.zeros_like(acc)
    starts = starts_ref[...]
    query = lax.broadcasted_iota(jnp.int32, (STEP * TOK, TOK), 1) + CHUNKS * TOK
    local = lax.broadcasted_iota(jnp.int32, (STEP * TOK, TOK), 0)

    def step(number, _):
        first = number * STEP
        pieces = []
        for i in range(STEP):
            w = place + first + i
            own = w >= CHUNKS
            chunk = jnp.where(own, w - CHUNKS, w)
            row = pl.multiple_of(jnp.where(own, 0, TOK), TOK)
            pieces.append(kv_ref.at[chunk, pl.ds(row, TOK), :])
        pos = local + first * TOK
        allowed = (pos >= starts) & (pos <= query)
        for g in range(KV_HEADS):
            keys = jnp.concatenate([p[:, g * HEAD : (g + 1) * HEAD] for p in pieces], axis=0)
            vals = jnp.concatenate(
                [p[:, (KV_HEADS + g) * HEAD : (KV_HEADS + g + 1) * HEAD] for p in pieces], axis=0
            )
            for h in range(group_heads):
                head = g * group_heads + h
                s = jnp.dot(keys, q_ref[head], preferred_element_type=F32) * scale
                s = jnp.where(allowed, s, NEG)
                old = top[head : head + 1, :]
                new = jnp.maximum(old, jnp.max(s, axis=0, keepdims=True))
                alpha = jnp.exp2(old - new)
                w = jnp.exp2(s - new)
                top[head : head + 1, :] = new
                total[head : head + 1, :] = total[head : head + 1, :] * alpha + jnp.sum(
                    w, axis=0, keepdims=True
                )
                got = lax.dot_general(
                    vals, w.astype(BF16), (((0,), (0,)), ((), ())), preferred_element_type=F32
                )
                acc[head] = acc[head] * alpha + got
        return 0

    lax.fori_loop(0, (CHUNKS + 1) // STEP, step, 0)
    for head in range(HEADS):
        out_ref[head] = (acc[head] / total[head : head + 1, :]).astype(BF16)


def attention(starts, q_t, kv_all):
    vm = pl.BlockSpec(memory_space=pltpu.VMEM)
    return pl.pallas_call(
        attention_kernel,
        out_shape=jax.ShapeDtypeStruct((HEADS, HEAD, TOK), BF16),
        in_specs=[vm, vm, vm],
        out_specs=vm,
        scratch_shapes=[
            pltpu.VMEM((16, TOK), F32),
            pltpu.VMEM((16, TOK), F32),
            pltpu.VMEM((HEADS, HEAD, TOK), F32),
        ],
        cost_estimate=pl.CostEstimate(
            flops=4 * HEADS * TOK * HEAD * (CHUNKS + 1) * TOK,
            bytes_accessed=kv_all.size * 2,
            transcendentals=HEADS * TOK * (CHUNKS + 1) * TOK,
        ),
        name="window_attention",
    )(starts, q_t, kv_all)


def body(
    tokens,
    segment_ids,
    page_table,
    attn_gain,
    w_qkv,
    w_out,
    moe_gain,
    route_ids,
    route_weight,
    w_gate,
    w_up,
    w_down,
):
    tok_rows = tokens.shape[0]
    tensor_size = lax.axis_size("tensor")
    tensor_index = lax.axis_index("tensor")
    seq_index = lax.axis_index("seq")
    seq_size = lax.axis_size("seq")
    query_width = HEADS * HEAD

    counts = jnp.sum(
        (segment_ids[:, None] < jnp.arange(TOK, dtype=jnp.int32)[None, :]).astype(F32), axis=0
    ).astype(BF16)
    counts_rows = jnp.pad(counts[None, :], ((0, PAGE - 1), (0, tokens.shape[1] - TOK)))
    sent = jnp.concatenate([tokens, counts_rows], axis=0)
    earlier = lax.ppermute(sent, "seq", [(i, i + 1) for i in range(seq_size - 1)])
    both = jnp.concatenate([tokens, earlier[:tok_rows]], axis=0)
    normed = rms_scaled(both, attn_gain)
    qkv_t = lax.all_gather(w_qkv.T, "tensor", axis=0, tiled=True)
    nt = (((1,), (1,)), ((), ()))
    q_t = lax.dot_general(
        qkv_t[:query_width], normed[:tok_rows], nt, preferred_element_type=F32
    ).astype(BF16)
    kv = lax.dot_general(normed, qkv_t[query_width:], nt, preferred_element_type=F32).astype(BF16)
    kvw = kv.shape[1]
    seg_rows = jnp.concatenate(
        [jnp.pad(counts[None, :], ((0, 0), (0, kvw - TOK))),
         jnp.pad(earlier[tok_rows:, :kvw], ((0, 0), (0, 0)))[: PAGE - 1]], axis=0
    )
    chunk = jnp.concatenate([kv, seg_rows], axis=0)
    kv_all = lax.all_gather(chunk, "tensor", axis=0, tiled=False)

    own_counts = kv_all[:, 2 * tok_rows, :TOK].astype(F32)
    prev_counts = kv_all[:, 2 * tok_rows + 1, :TOK].astype(F32)
    order = jnp.arange(tensor_size)[:, None]
    before = jnp.where(seq_index == 0, jnp.full_like(prev_counts, TOK), prev_counts)
    starts_of = jnp.sum(
        jnp.where(order <= tensor_index, own_counts, 0.0)
        + jnp.where(order >= tensor_index, before, 0.0),
        axis=0,
    ).astype(jnp.int32)
    starts = jnp.sum(
        jnp.where(
            segment_ids[None, :] == jnp.arange(TOK, dtype=jnp.int32)[:, None], starts_of[:, None], 0
        ),
        axis=0,
    )
    ctx = attention(starts[None, :], q_t.reshape(HEADS, HEAD, tok_rows), kv_all)

    pages_here = tok_rows // PAGE
    pages_block = page_table.shape[1]
    slot_ids = tensor_index * pages_here + jnp.arange(pages_here, dtype=jnp.int32)
    matches = page_table[0][None, :] == slot_ids[:, None]
    logical = jnp.sum(
        jnp.where(matches, jnp.arange(pages_block, dtype=jnp.int32)[None, :], 0), axis=1
    )
    cache_pages = jnp.stack(
        [
            lax.dynamic_slice(
                kv_all,
                (logical[i] // pages_here, (logical[i] % pages_here) * PAGE, 0),
                (1, PAGE, kvw),
            )[0]
            for i in range(pages_here)
        ]
    )

    held, _ = lax.optimization_barrier((w_out, kv))
    out_t = lax.all_gather(held.T, "tensor", axis=0, tiled=True)
    attn_out = lax.dot_general(
        ctx.reshape(query_width, tok_rows), out_t, (((0,), (1,)), ((), ())),
        preferred_element_type=F32,
    )
    residual = (tokens.astype(F32) + attn_out).astype(BF16)
    expert_input = rms_scaled(residual, moe_gain)

    experts_all = w_gate.shape[0] * tensor_size
    capacity = max(2, 3 * tok_rows * TOP // (2 * experts_all))
    flat_routes = route_ids.reshape(-1)
    expert_hits = (
        flat_routes[:, None] == jnp.arange(experts_all, dtype=jnp.int32)[None, :]
    ).astype(jnp.int32)
    earlier_hits = jnp.cumsum(expert_hits, axis=0) - expert_hits
    slot_rank = jnp.sum(earlier_hits * expert_hits, axis=1)
    dest_slot = (flat_routes * capacity + slot_rank).reshape(tok_rows, TOP)
    slot_table = (
        jnp.arange(experts_all * capacity, dtype=jnp.int32)[:, None, None] == dest_slot[None]
    )
    dispatch = jnp.any(slot_table, axis=2).astype(BF16)
    spread = jnp.sum(
        jnp.where(
            jnp.arange(experts_all * capacity, dtype=jnp.int32)[None, :, None]
            == dest_slot[:, None, :],
            route_weight[:, None, :],
            0.0,
        ),
        axis=2,
    )
    high = spread.astype(BF16)
    low = (spread - high.astype(F32)).astype(BF16)
    outgoing = jnp.dot(dispatch, expert_input, preferred_element_type=F32).astype(BF16)
    outgoing = outgoing.reshape(experts_all, capacity, expert_input.shape[1])
    arrived = lax.all_to_all(outgoing, "tensor", split_axis=0, concat_axis=0, tiled=True)
    rows_flat = arrived.reshape(-1, arrived.shape[-1])
    gate_out = jnp.dot(rows_flat, w_gate[0], preferred_element_type=F32)
    up_out = jnp.dot(rows_flat, w_up[0], preferred_element_type=F32)
    hidden = (jnp.maximum(gate_out, 0.0) * up_out).astype(BF16)
    produced = jnp.dot(hidden, w_down[0], preferred_element_type=F32).astype(BF16)
    returned = lax.all_to_all(
        produced.reshape(arrived.shape), "tensor", split_axis=0, concat_axis=0, tiled=True
    ).reshape(rows_flat.shape)
    routed_sum = jnp.dot(high, returned, preferred_element_type=F32) + jnp.dot(
        low, returned, preferred_element_type=F32
    )
    mixed = (residual.astype(F32) + routed_sum).astype(BF16)
    return (mixed, cache_pages)


def solution(mesh):
    return jax.shard_map(
        body,
        mesh=mesh,
        in_specs=(
            P(("seq", "tensor"), None),
            P(("seq", "tensor")),
            P("seq", None),
            P(),
            P(None, "tensor"),
            P(None, "tensor"),
            P(),
            P(("seq", "tensor"), None),
            P(("seq", "tensor"), None),
            P("tensor", None, None),
            P("tensor", None, None),
            P("tensor", None, None),
        ),
        out_specs=(P(("seq", "tensor"), None), P(("seq", "tensor"), None, None)),
        check_vma=False,
    )
```

```python
import functools
import math

import jax
import jax.numpy as jnp
from jax import lax
from jax.experimental import pallas as pl
from jax.experimental.pallas import tpu as pltpu
from jax.sharding import PartitionSpec as P

HEADS = 12
KV_HEADS = 2
HEAD = 128
TOP = 4
PAGE = 16
SEGS = 32
CHUNKS = 32
TOK = 128
STEP = 3
NEG = -1e30

epsilon = 1e-06
F32 = jnp.float32
BF16 = jnp.bfloat16


def rms_scaled(values, scales):
    wide = values.astype(F32)
    mean_sq = jnp.mean(wide * wide, axis=-1, keepdims=True)
    return (wide * lax.rsqrt(mean_sq + epsilon) * scales).astype(BF16)


def attention_kernel(starts_ref, q_ref, kv_ref, out_ref, top, total, acc):
    place = lax.axis_index("tensor")
    scale = math.log2(math.e) / math.sqrt(HEAD)
    group_heads = HEADS // KV_HEADS
    top[...] = jnp.full_like(top, NEG)
    total[...] = jnp.zeros_like(total)
    acc[...] = jnp.zeros_like(acc)
    starts = starts_ref[...]
    query = lax.broadcasted_iota(jnp.int32, (STEP * TOK, TOK), 1) + CHUNKS * TOK
    local = lax.broadcasted_iota(jnp.int32, (STEP * TOK, TOK), 0)

    def step(number, _):
        first = number * STEP
        pieces = []
        for i in range(STEP):
            w = place + first + i
            own = w >= CHUNKS
            chunk = jnp.where(own, w - CHUNKS, w)
            row = pl.multiple_of(jnp.where(own, 0, TOK), TOK)
            pieces.append(kv_ref.at[chunk, pl.ds(row, TOK), :])
        pos = local + first * TOK
        allowed = (pos >= starts) & (pos <= query)
        for g in range(KV_HEADS):
            keys = jnp.concatenate([p[:, g * HEAD : (g + 1) * HEAD] for p in pieces], axis=0)
            vals = jnp.concatenate(
                [p[:, (KV_HEADS + g) * HEAD : (KV_HEADS + g + 1) * HEAD] for p in pieces], axis=0
            )
            for h in range(group_heads):
                head = g * group_heads + h
                s = jnp.dot(keys, q_ref[head], preferred_element_type=F32) * scale
                s = jnp.where(allowed, s, NEG)
                old = top[head : head + 1, :]
                new = jnp.maximum(old, jnp.max(s, axis=0, keepdims=True))
                alpha = jnp.exp2(old - new)
                w = jnp.exp2(s - new)
                top[head : head + 1, :] = new
                total[head : head + 1, :] = total[head : head + 1, :] * alpha + jnp.sum(
                    w, axis=0, keepdims=True
                )
                got = lax.dot_general(
                    vals, w.astype(BF16), (((0,), (0,)), ((), ())), preferred_element_type=F32
                )
                acc[head] = acc[head] * alpha + got
        return 0

    lax.fori_loop(0, (CHUNKS + 1) // STEP, step, 0)
    for head in range(HEADS):
        out_ref[head] = (acc[head] / total[head : head + 1, :]).astype(BF16)


RING = 4
FULL_A, HALF_A, FULL_B, HALF_B, PAIR = 0, 2, 4, 12, 20
COPIES = 36
ORDER = (0, -1, 1, 2)


def gather_kernel(splits, with_seq, *refs):
    count = len(splits)
    refs = list(refs)
    shards = refs[:count]
    refs = refs[count:]
    if with_seq:
        sent_ref = refs.pop(0)
    outs = refs[:count]
    refs = refs[count:]
    if with_seq:
        got_ref = refs.pop(0)
    send, recv, here = refs[:3]
    place = lax.axis_index("tensor")
    core = lax.rem(place, 2)
    px = lax.rem(place // 2, RING)
    py = place // (2 * RING)

    def at(a, b, flip=0):
        x = lax.rem(px + a * (1 - core) + b * core + RING, RING)
        y = lax.rem(py + a * core + b * (1 - core) + RING, RING)
        c = (1 - core) if flip else core
        return (y * RING + x) * 2 + c

    barrier = pltpu.get_barrier_semaphore()
    peers = [at(1, 0), at(-1, 0), at(0, 1), at(0, -1), at(0, 0, 1)]
    for peer in peers:
        pl.semaphore_signal(
            barrier, inc=1, device_id={"tensor": peer}, device_id_type=pl.DeviceIdType.MESH
        )
    if with_seq:
        seq = lax.axis_index("seq")
        seq_size = lax.axis_size("seq")
        later = lax.rem(seq + 1, seq_size)
        for peer in (later, lax.rem(seq + seq_size - 1, seq_size)):
            pl.semaphore_signal(
                barrier, inc=1, device_id={"seq": peer}, device_id_type=pl.DeviceIdType.MESH
            )
    pl.semaphore_wait(barrier, 7 if with_seq else 5)

    def view(n, a, b, part):
        ref = outs[n].at[at(a, b)]
        if part is None:
            return ref
        axis, cut = splits[n]
        rows, cols = outs[n].shape[1:]
        whole = rows if axis == 0 else cols
        span = pl.ds(0, cut) if part == 0 else pl.ds(cut, whole - cut)
        return ref.at[span, :] if axis == 0 else ref.at[:, span]

    def copy(n, kind, a, b, part, target):
        src = shards[n] if (a == 0 and b == 0) else view(n, a, b, part)
        return pltpu.make_async_remote_copy(
            src_ref=src,
            dst_ref=view(n, a, b, part),
            send_sem=send.at[n, kind],
            recv_sem=recv.at[n, kind],
            device_id={"tensor": target},
            device_id_type=pl.DeviceIdType.MESH,
        )

    started = []

    def go(n, kind, a, b, part, target):
        c = copy(n, kind, a, b, part, target)
        c.start()
        started.append(c)

    def landed(n, kind, a, b, part):
        copy(n, kind, a, b, part, at(0, 0, 1)).wait_recv()

    def spread(n, k):
        r = ORDER[k]
        go(n, FULL_B + 2 * k, r, 0, None, at(0, 1))
        go(n, FULL_B + 2 * k + 1, r, 0, None, at(0, -1))
        go(n, PAIR + k, r, 0, None, at(0, 0, 1))

    own = []
    for n in range(count):
        go(n, FULL_A, 0, 0, None, at(1, 0))
        go(n, FULL_A + 1, 0, 0, None, at(-1, 0))
        spread(n, 0)
    for n in range(count):
        c = pltpu.make_async_copy(shards[n], outs[n].at[place], here.at[n])
        c.start()
        own.append(c)
    if with_seq:
        z = pltpu.make_async_remote_copy(
            src_ref=sent_ref,
            dst_ref=got_ref,
            send_sem=here.at[count],
            recv_sem=here.at[count + 1],
            device_id={"seq": later},
            device_id_type=pl.DeviceIdType.MESH,
        )
        z.start()
    for n in range(count):
        landed(n, FULL_A, -1, 0, None)
        go(n, HALF_A, -1, 0, 0, at(1, 0))
        spread(n, 1)
        landed(n, FULL_A + 1, 1, 0, None)
        go(n, HALF_A + 1, 1, 0, 1, at(-1, 0))
        spread(n, 2)
    for n in range(count):
        for k in (0, 1, 2, 3):
            r = ORDER[k]
            if k == 1:
                landed(n, HALF_A, 2, 0, 0)
                landed(n, HALF_A + 1, 2, 0, 1)
                spread(n, 3)
            landed(n, FULL_B + 2 * k, r, -1, None)
            go(n, HALF_B + 2 * k, r, -1, 0, at(0, 1))
            go(n, PAIR + 4 + k, r, -1, None, at(0, 0, 1))
            landed(n, FULL_B + 2 * k + 1, r, 1, None)
            go(n, HALF_B + 2 * k + 1, r, 1, 1, at(0, -1))
            go(n, PAIR + 8 + k, r, 1, None, at(0, 0, 1))
    for n in range(count):
        for k in range(RING):
            landed(n, HALF_B + 2 * k, ORDER[k], 2, 0)
            landed(n, HALF_B + 2 * k + 1, ORDER[k], 2, 1)
            go(n, PAIR + 12 + k, ORDER[k], 2, None, at(0, 0, 1))
    for c in own:
        c.wait()
    if with_seq:
        z.wait()
    for n in range(count):
        for k in range(4 * RING):
            pltpu.make_async_remote_copy(
                src_ref=outs[n].at[place],
                dst_ref=outs[n].at[place],
                send_sem=send.at[n, PAIR + k],
                recv_sem=recv.at[n, PAIR + k],
                device_id={"tensor": at(0, 0, 1)},
                device_id_type=pl.DeviceIdType.MESH,
            ).wait_recv()
    for c in started:
        c.wait_send()


def gather(shards, splits, number, sent=None):
    places = lax.axis_size("tensor")
    vm = pl.BlockSpec(memory_space=pltpu.VMEM)
    anyspace = pl.BlockSpec(memory_space=pl.ANY)
    with_seq = sent is not None
    out_shape = [jax.ShapeDtypeStruct((places,) + s.shape, s.dtype) for s in shards]
    args = list(shards)
    out_specs = [anyspace] * len(shards)
    if with_seq:
        args.append(sent)
        out_shape.append(jax.ShapeDtypeStruct(sent.shape, sent.dtype))
        out_specs.append(vm)
    return pl.pallas_call(
        functools.partial(gather_kernel, splits, with_seq),
        out_shape=out_shape,
        in_specs=[vm] * len(args),
        out_specs=out_specs,
        scratch_shapes=[
            pltpu.SemaphoreType.DMA((len(shards), COPIES)),
            pltpu.SemaphoreType.DMA((len(shards), COPIES)),
            pltpu.SemaphoreType.DMA((len(shards) + 2,)),
        ],
        compiler_params=pltpu.CompilerParams(collective_id=number, has_side_effects=True),
        name="gather_%d" % number,
    )(*args)


def attention(starts, q_t, kv_all):
    vm = pl.BlockSpec(memory_space=pltpu.VMEM)
    return pl.pallas_call(
        attention_kernel,
        out_shape=jax.ShapeDtypeStruct((HEADS, HEAD, TOK), BF16),
        in_specs=[vm, vm, vm],
        out_specs=vm,
        scratch_shapes=[
            pltpu.VMEM((16, TOK), F32),
            pltpu.VMEM((16, TOK), F32),
            pltpu.VMEM((HEADS, HEAD, TOK), F32),
        ],
        cost_estimate=pl.CostEstimate(
            flops=4 * HEADS * TOK * HEAD * (CHUNKS + 1) * TOK,
            bytes_accessed=kv_all.size * 2,
            transcendentals=HEADS * TOK * (CHUNKS + 1) * TOK,
        ),
        name="window_attention",
    )(starts, q_t, kv_all)


def body(
    tokens,
    segment_ids,
    page_table,
    attn_gain,
    w_qkv,
    w_out,
    moe_gain,
    route_ids,
    route_weight,
    w_gate,
    w_up,
    w_down,
):
    tok_rows = tokens.shape[0]
    tensor_size = lax.axis_size("tensor")
    tensor_index = lax.axis_index("tensor")
    seq_index = lax.axis_index("seq")
    query_width = HEADS * HEAD

    counts = jnp.sum(
        (segment_ids[:, None] < jnp.arange(TOK, dtype=jnp.int32)[None, :]).astype(F32), axis=0
    ).astype(BF16)
    counts_rows = jnp.pad(counts[None, :], ((0, PAGE - 1), (0, tokens.shape[1] - TOK)))
    sent = jnp.concatenate([tokens, counts_rows], axis=0)
    qkv_t, earlier = gather([w_qkv.T], [(0, w_qkv.shape[1] // 2)], 0, sent)
    qkv_t = qkv_t.reshape(-1, tokens.shape[1])
    both = jnp.concatenate([tokens, earlier[:tok_rows]], axis=0)
    normed = rms_scaled(both, attn_gain)
    nt = (((1,), (1,)), ((), ()))
    q_t = lax.dot_general(
        qkv_t[:query_width], normed[:tok_rows], nt, preferred_element_type=F32
    ).astype(BF16)
    kv = lax.dot_general(normed, qkv_t[query_width:], nt, preferred_element_type=F32).astype(BF16)
    kvw = kv.shape[1]
    seg_rows = jnp.concatenate(
        [jnp.pad(counts[None, :], ((0, 0), (0, kvw - TOK))),
         jnp.pad(earlier[tok_rows:, :kvw], ((0, 0), (0, 0)))[: PAGE - 1]], axis=0
    )
    chunk = jnp.concatenate([kv, seg_rows], axis=0)
    kv_all, out_t = gather(
        [chunk, w_out.T], [(0, tok_rows + PAGE), (1, query_width // 2)], 1
    )
    out_t = out_t.reshape(-1, query_width)

    own_counts = kv_all[:, 2 * tok_rows, :TOK].astype(F32)
    prev_counts = kv_all[:, 2 * tok_rows + 1, :TOK].astype(F32)
    order = jnp.arange(tensor_size)[:, None]
    before = jnp.where(seq_index == 0, jnp.full_like(prev_counts, TOK), prev_counts)
    starts_of = jnp.sum(
        jnp.where(order <= tensor_index, own_counts, 0.0)
        + jnp.where(order >= tensor_index, before, 0.0),
        axis=0,
    ).astype(jnp.int32)
    starts = jnp.sum(
        jnp.where(
            segment_ids[None, :] == jnp.arange(TOK, dtype=jnp.int32)[:, None], starts_of[:, None], 0
        ),
        axis=0,
    )
    ctx = attention(starts[None, :], q_t.reshape(HEADS, HEAD, tok_rows), kv_all)

    pages_here = tok_rows // PAGE
    pages_block = page_table.shape[1]
    slot_ids = tensor_index * pages_here + jnp.arange(pages_here, dtype=jnp.int32)
    matches = page_table[0][None, :] == slot_ids[:, None]
    logical = jnp.sum(
        jnp.where(matches, jnp.arange(pages_block, dtype=jnp.int32)[None, :], 0), axis=1
    )
    cache_pages = jnp.stack(
        [
            lax.dynamic_slice(
                kv_all,
                (logical[i] // pages_here, (logical[i] % pages_here) * PAGE, 0),
                (1, PAGE, kvw),
            )[0]
            for i in range(pages_here)
        ]
    )

    attn_out = lax.dot_general(
        ctx.reshape(query_width, tok_rows), out_t, (((0,), (1,)), ((), ())),
        preferred_element_type=F32,
    )
    residual = (tokens.astype(F32) + attn_out).astype(BF16)
    expert_input = rms_scaled(residual, moe_gain)

    experts_all = w_gate.shape[0] * tensor_size
    capacity = max(2, 3 * tok_rows * TOP // (2 * experts_all))
    picks = route_ids.T[None] == jnp.arange(experts_all, dtype=jnp.int32)[:, None, None]
    hits = jnp.any(picks, axis=1)
    weights = jnp.sum(jnp.where(picks, route_weight.T[None], 0.0), axis=1)
    order_of = jnp.arange(tok_rows, dtype=jnp.int32)
    ahead = (order_of[:, None] < order_of[None, :]).astype(BF16)
    ranks = jnp.dot(hits.astype(BF16), ahead, preferred_element_type=F32)
    slots = jnp.arange(capacity, dtype=jnp.int32).astype(F32)[None, :, None]
    taken = jnp.logical_and(hits[:, None, :], ranks[:, None, :] == slots)
    dispatch = taken.astype(BF16).reshape(experts_all * capacity, tok_rows)
    spread = jnp.where(taken, weights[:, None, :], 0.0).reshape(experts_all * capacity, tok_rows)
    high = spread.astype(BF16)
    low = (spread - high.astype(F32)).astype(BF16)
    outgoing = jnp.dot(dispatch, expert_input, preferred_element_type=F32).astype(BF16)
    outgoing = outgoing.reshape(experts_all, capacity, expert_input.shape[1])
    arrived = lax.all_to_all(outgoing, "tensor", split_axis=0, concat_axis=0, tiled=True)
    rows_flat = arrived.reshape(-1, arrived.shape[-1])
    gate_out = jnp.dot(rows_flat, w_gate[0], preferred_element_type=F32)
    up_out = jnp.dot(rows_flat, w_up[0], preferred_element_type=F32)
    hidden = (jnp.maximum(gate_out, 0.0) * up_out).astype(BF16)
    produced = jnp.dot(hidden, w_down[0], preferred_element_type=F32).astype(BF16)
    returned = lax.all_to_all(
        produced.reshape(arrived.shape), "tensor", split_axis=0, concat_axis=0, tiled=True
    ).reshape(rows_flat.shape)
    tn = (((0,), (0,)), ((), ()))
    routed_sum = lax.dot_general(
        high, returned, tn, preferred_element_type=F32
    ) + lax.dot_general(low, returned, tn, preferred_element_type=F32)
    mixed = (residual.astype(F32) + routed_sum).astype(BF16)
    return (mixed, cache_pages)


def solution(mesh):
    return jax.shard_map(
        body,
        mesh=mesh,
        in_specs=(
            P(("seq", "tensor"), None),
            P(("seq", "tensor")),
            P("seq", None),
            P(),
            P(None, "tensor"),
            P(None, "tensor"),
            P(),
            P(("seq", "tensor"), None),
            P(("seq", "tensor"), None),
            P("tensor", None, None),
            P("tensor", None, None),
            P("tensor", None, None),
        ),
        out_specs=(P(("seq", "tensor"), None), P(("seq", "tensor"), None, None)),
        check_vma=False,
    )
```

```python
import functools
import math

import jax
import jax.numpy as jnp
from jax import lax
from jax.experimental import pallas as pl
from jax.experimental.pallas import tpu as pltpu
from jax.sharding import PartitionSpec as P

HEADS = 12
KV_HEADS = 2
HEAD = 128
TOP = 4
PAGE = 16
SEGS = 32
CHUNKS = 32
TOK = 128
STEP = 3
NEG = -1e30

epsilon = 1e-06
F32 = jnp.float32
BF16 = jnp.bfloat16


def rms_scaled(values, scales):
    wide = values.astype(F32)
    mean_sq = jnp.mean(wide * wide, axis=-1, keepdims=True)
    return (wide * lax.rsqrt(mean_sq + epsilon) * scales).astype(BF16)


RING = 4
FULL_A, HALF_A, FULL_B, HALF_B, PAIR = 0, 2, 4, 12, 20
COPIES = 36
ORDER = (0, -1, 1, 2)
MESH = pl.DeviceIdType.MESH


class Rings:
    def __init__(self, shards, outs, splits, send, recv, here):
        self.shards, self.outs, self.splits = shards, outs, splits
        self.send, self.recv, self.here = send, recv, here
        self.place = lax.axis_index("tensor")
        self.core = lax.rem(self.place, 2)
        self.px = lax.rem(self.place // 2, RING)
        self.py = self.place // (2 * RING)
        self.started = []
        self.every = range(len(shards))

    def at(self, a, b, flip=0):
        core = self.core
        x = lax.rem(self.px + a * (1 - core) + b * core + RING, RING)
        y = lax.rem(self.py + a * core + b * (1 - core) + RING, RING)
        return (y * RING + x) * 2 + ((1 - core) if flip else core)

    def greet(self, barrier):
        for where in ((1, 0), (-1, 0), (0, 1), (0, -1), (0, 0, 1)):
            pl.semaphore_signal(
                barrier, inc=1, device_id={"tensor": self.at(*where)}, device_id_type=MESH
            )
        return 5

    def view(self, n, a, b, part):
        ref = self.outs[n].at[self.at(a, b)]
        if part is None:
            return ref
        axis, cut = self.splits[n]
        whole = self.outs[n].shape[1 + axis]
        span = pl.ds(0, cut) if part == 0 else pl.ds(cut, whole - cut)
        return ref.at[span, :] if axis == 0 else ref.at[:, span]

    def copy(self, n, kind, a, b, part, where):
        src = self.shards[n] if (a == 0 and b == 0) else self.view(n, a, b, part)
        return pltpu.make_async_remote_copy(
            src_ref=src,
            dst_ref=self.view(n, a, b, part),
            send_sem=self.send.at[n, kind],
            recv_sem=self.recv.at[n, kind],
            device_id={"tensor": self.at(*where)},
            device_id_type=MESH,
        )

    def go(self, *what):
        self.copy(*what).start()
        self.started.append(what)

    def landed(self, n, kind, a, b, part):
        self.copy(n, kind, a, b, part, (0, 0, 1)).wait_recv()

    def spread(self, n, k):
        r = ORDER[k]
        self.go(n, FULL_B + 2 * k, r, 0, None, (0, 1))
        self.go(n, FULL_B + 2 * k + 1, r, 0, None, (0, -1))
        self.go(n, PAIR + k, r, 0, None, (0, 0, 1))

    def own(self, n):
        return pltpu.make_async_copy(
            self.shards[n], self.outs[n].at[self.place], self.here.at[n]
        )

    def begin(self):
        for n in self.every:
            self.go(n, FULL_A, 0, 0, None, (1, 0))
            self.go(n, FULL_A + 1, 0, 0, None, (-1, 0))
            self.spread(n, 0)
        for n in self.every:
            self.own(n).start()

    def first_ring(self):
        for n in self.every:
            self.landed(n, FULL_A, -1, 0, None)
            self.go(n, HALF_A, -1, 0, 0, (1, 0))
            self.spread(n, 1)
            self.landed(n, FULL_A + 1, 1, 0, None)
            self.go(n, HALF_A + 1, 1, 0, 1, (-1, 0))
            self.spread(n, 2)

    def second_ring(self, k):
        r = ORDER[k]
        for n in self.every:
            if k == 1:
                self.landed(n, HALF_A, 2, 0, 0)
                self.landed(n, HALF_A + 1, 2, 0, 1)
                self.spread(n, 3)
            self.landed(n, FULL_B + 2 * k, r, -1, None)
            self.go(n, HALF_B + 2 * k, r, -1, 0, (0, 1))
            self.go(n, PAIR + 4 + k, r, -1, None, (0, 0, 1))
            self.landed(n, FULL_B + 2 * k + 1, r, 1, None)
            self.go(n, HALF_B + 2 * k + 1, r, 1, 1, (0, -1))
            self.go(n, PAIR + 8 + k, r, 1, None, (0, 0, 1))

    def last(self):
        for n in self.every:
            for k in range(RING):
                self.landed(n, HALF_B + 2 * k, ORDER[k], 2, 0)
                self.landed(n, HALF_B + 2 * k + 1, ORDER[k], 2, 1)
                self.go(n, PAIR + 12 + k, ORDER[k], 2, None, (0, 0, 1))

    def finish(self):
        for n in self.every:
            self.own(n).wait()
            for k in range(4 * RING):
                self.landed(n, PAIR + k, 1, 1, None)
        for what in self.started:
            self.copy(*what).wait_send()


def ring_scratch(count):
    return [
        pltpu.SemaphoreType.DMA((count, COPIES)),
        pltpu.SemaphoreType.DMA((count, COPIES)),
        pltpu.SemaphoreType.DMA((count,)),
    ]


def gather_kernel(splits, extra, *refs):
    count = len(splits)
    shards, refs = refs[:count], refs[count:]
    sent, refs = refs[:extra], refs[extra:]
    outs, refs = refs[:count], refs[count:]
    got, refs = refs[:extra], refs[extra:]
    rings = Rings(shards, outs, splits, *refs[:3])
    barrier = pltpu.get_barrier_semaphore()
    greeted = rings.greet(barrier)
    steps = []
    if extra:
        seq = lax.axis_index("seq")
        seq_size = lax.axis_size("seq")
        later = lax.rem(seq + 1, seq_size)
        for peer in (later, lax.rem(seq + seq_size - 1, seq_size)):
            pl.semaphore_signal(barrier, inc=1, device_id={"seq": peer}, device_id_type=MESH)
        greeted += 2
    pl.semaphore_wait(barrier, greeted)
    rings.begin()
    for i in range(extra):
        z = pltpu.make_async_remote_copy(
            src_ref=sent[i],
            dst_ref=got[i],
            send_sem=refs[3].at[2 * i],
            recv_sem=refs[3].at[2 * i + 1],
            device_id={"seq": later},
            device_id_type=MESH,
        )
        z.start()
        steps.append(z)
    rings.first_ring()
    for k in range(RING):
        rings.second_ring(k)
    rings.last()
    for z in steps:
        z.wait()
    rings.finish()


def gather(shards, splits, number, sent=()):
    places = lax.axis_size("tensor")
    vm = pl.BlockSpec(memory_space=pltpu.VMEM)
    anyspace = pl.BlockSpec(memory_space=pl.ANY)
    return pl.pallas_call(
        functools.partial(gather_kernel, splits, len(sent)),
        out_shape=[jax.ShapeDtypeStruct((places,) + s.shape, s.dtype) for s in shards]
        + [jax.ShapeDtypeStruct(s.shape, s.dtype) for s in sent],
        in_specs=[vm] * (len(shards) + len(sent)),
        out_specs=[anyspace] * len(shards) + [vm] * len(sent),
        scratch_shapes=ring_scratch(len(shards))
        + ([pltpu.SemaphoreType.DMA((2 * len(sent),))] if sent else []),
        compiler_params=pltpu.CompilerParams(collective_id=number, has_side_effects=True),
        name="gather_%d" % number,
    )(*shards, *sent)


def attention_kernel(
    starts_ref, q_ref, w_ref, kv_ref, out_ref, gathered_ref, kv, top, total, acc, chunk_sem, *sems
):
    place = lax.axis_index("tensor")
    rings = Rings([w_ref], [gathered_ref], [(1, w_ref.shape[1] // 2)], *sems)
    barrier = pltpu.get_barrier_semaphore()
    greeted = rings.greet(barrier)

    def fetch(i):
        w = place + i
        block = w // CHUNKS
        row = pl.multiple_of((1 - block) * TOK, TOK)
        return pltpu.make_async_copy(
            kv_ref.at[w - block * CHUNKS, pl.ds(row, TOK), :], kv.at[i], chunk_sem.at[i]
        )

    def fetch_step(i, _):
        fetch(i).start()
        return 0

    lax.fori_loop(0, CHUNKS + 1, fetch_step, 0)
    scale = math.log2(math.e) / math.sqrt(HEAD)
    group_heads = HEADS // KV_HEADS
    top[...] = jnp.full_like(top, NEG)
    total[...] = jnp.zeros_like(total)
    acc[...] = jnp.zeros_like(acc)
    pl.semaphore_wait(barrier, greeted)
    rings.begin()
    starts = starts_ref[...]
    query = lax.broadcasted_iota(jnp.int32, (STEP * TOK, TOK), 1) + CHUNKS * TOK
    local = lax.broadcasted_iota(jnp.int32, (STEP * TOK, TOK), 0)

    def step(number, _):
        first = number * STEP
        pl.when(number == 2)(rings.first_ring)
        for k in range(RING):
            pl.when(number == 3 + k)(functools.partial(rings.second_ring, k))
        pl.when(number == 8)(rings.last)
        for i in range(STEP):
            fetch(first + i).wait()
        pieces = [kv.at[first + i] for i in range(STEP)]
        pos = local + first * TOK
        allowed = (pos >= starts) & (pos <= query)
        for g in range(KV_HEADS):
            keys = jnp.concatenate([p[:, g * HEAD : (g + 1) * HEAD] for p in pieces], axis=0)
            vals = jnp.concatenate(
                [p[:, (KV_HEADS + g) * HEAD : (KV_HEADS + g + 1) * HEAD] for p in pieces], axis=0
            )
            for h in range(group_heads):
                head = g * group_heads + h
                s = lax.dot_general(
                    keys,
                    q_ref[:, head * HEAD : (head + 1) * HEAD],
                    (((1,), (1,)), ((), ())),
                    preferred_element_type=F32,
                )
                s = jnp.where(allowed, s * scale, NEG)
                old = top[head : head + 1, :]
                new = jnp.maximum(old, jnp.max(s, axis=0, keepdims=True))
                alpha = jnp.exp2(old - new)
                w = jnp.exp2(s - new)
                top[head : head + 1, :] = new
                total[head : head + 1, :] = total[head : head + 1, :] * alpha + jnp.sum(
                    w, axis=0, keepdims=True
                )
                got = lax.dot_general(
                    vals, w.astype(BF16), (((0,), (0,)), ((), ())), preferred_element_type=F32
                )
                acc[head] = acc[head] * alpha + got
        return 0

    lax.fori_loop(0, (CHUNKS + 1) // STEP, step, 0)
    for head in range(HEADS):
        out_ref[head] = (acc[head] / total[head : head + 1, :]).astype(BF16)
    rings.finish()


def attention(starts, q, w_out_t, kv_all):
    vm = pl.BlockSpec(memory_space=pltpu.VMEM)
    anyspace = pl.BlockSpec(memory_space=pl.ANY)
    return pl.pallas_call(
        attention_kernel,
        out_shape=[
            jax.ShapeDtypeStruct((HEADS, HEAD, TOK), BF16),
            jax.ShapeDtypeStruct((CHUNKS,) + w_out_t.shape, BF16),
        ],
        in_specs=[vm, vm, vm, anyspace],
        out_specs=[vm, anyspace],
        scratch_shapes=[
            pltpu.VMEM((CHUNKS + 1, TOK, kv_all.shape[2]), BF16),
            pltpu.VMEM((16, TOK), F32),
            pltpu.VMEM((16, TOK), F32),
            pltpu.VMEM((HEADS, HEAD, TOK), F32),
            pltpu.SemaphoreType.DMA((CHUNKS + 1,)),
        ]
        + ring_scratch(1),
        compiler_params=pltpu.CompilerParams(collective_id=2, has_side_effects=True),
        name="window_attention",
    )(starts, q, w_out_t, kv_all)


def body(
    tokens,
    segment_ids,
    page_table,
    attn_gain,
    w_qkv,
    w_out,
    moe_gain,
    route_ids,
    route_weight,
    w_gate,
    w_up,
    w_down,
):
    tok_rows = tokens.shape[0]
    tensor_size = lax.axis_size("tensor")
    tensor_index = lax.axis_index("tensor")
    seq_index = lax.axis_index("seq")
    query_width = HEADS * HEAD

    counts = jnp.sum(
        (segment_ids[:, None] < jnp.arange(TOK, dtype=jnp.int32)[None, :]).astype(F32), axis=0
    ).astype(BF16)
    count_rows = jnp.broadcast_to(counts[None, :], (PAGE, TOK))
    qkv_t, earlier, earlier_counts = gather(
        [w_qkv.T], [(0, w_qkv.shape[1] // 2)], 0, (tokens, count_rows)
    )
    qkv_t = qkv_t.reshape(-1, tokens.shape[1])
    normed = rms_scaled(jnp.concatenate([tokens, earlier], axis=0), attn_gain)
    nt = (((1,), (1,)), ((), ()))
    projected = lax.dot_general(normed, qkv_t, nt, preferred_element_type=F32).astype(BF16)
    kv = projected[:, query_width:]
    kvw = kv.shape[1]
    upper = jnp.arange(2 * PAGE)[:, None] < PAGE
    both_counts = jnp.where(
        upper, jnp.tile(count_rows, (2, 1)), jnp.tile(earlier_counts, (2, 1))
    )
    kv_all, counts_all = gather([kv, both_counts], [(0, tok_rows), (0, PAGE)], 1)

    own_counts = counts_all[:, 0, :].astype(F32)
    prev_counts = counts_all[:, PAGE, :].astype(F32)
    order = jnp.arange(tensor_size)[:, None]
    before = jnp.where(seq_index == 0, jnp.full_like(prev_counts, TOK), prev_counts)
    starts_of = jnp.sum(
        jnp.where(order <= tensor_index, own_counts, 0.0)
        + jnp.where(order >= tensor_index, before, 0.0),
        axis=0,
    ).astype(jnp.int32)
    starts = jnp.sum(
        jnp.where(
            segment_ids[None, :] == jnp.arange(TOK, dtype=jnp.int32)[:, None], starts_of[:, None], 0
        ),
        axis=0,
    )
    ctx, out_t = attention(
        starts[None, :], projected[:tok_rows, :query_width], w_out.T, kv_all
    )
    out_t = out_t.reshape(-1, query_width)

    pages_here = tok_rows // PAGE
    pages_block = page_table.shape[1]
    slot_ids = tensor_index * pages_here + jnp.arange(pages_here, dtype=jnp.int32)
    matches = page_table[0][None, :] == slot_ids[:, None]
    logical = jnp.sum(
        jnp.where(matches, jnp.arange(pages_block, dtype=jnp.int32)[None, :], 0), axis=1
    )
    cache_pages = jnp.stack(
        [
            lax.dynamic_slice(
                kv_all,
                (logical[i] // pages_here, (logical[i] % pages_here) * PAGE, 0),
                (1, PAGE, kvw),
            )[0]
            for i in range(pages_here)
        ]
    )

    attn_out = lax.dot_general(
        ctx.reshape(query_width, tok_rows), out_t, (((0,), (1,)), ((), ())),
        preferred_element_type=F32,
    )
    residual = (tokens.astype(F32) + attn_out).astype(BF16)
    expert_input = rms_scaled(residual, moe_gain)

    experts_all = w_gate.shape[0] * tensor_size
    capacity = max(2, 3 * tok_rows * TOP // (2 * experts_all))
    picks = route_ids.T[None] == jnp.arange(experts_all, dtype=jnp.int32)[:, None, None]
    hits = jnp.any(picks, axis=1)
    weights = jnp.sum(jnp.where(picks, route_weight.T[None], 0.0), axis=1)
    order_of = jnp.arange(tok_rows, dtype=jnp.int32)
    ahead = (order_of[:, None] < order_of[None, :]).astype(BF16)
    ranks = jnp.dot(hits.astype(BF16), ahead, preferred_element_type=F32)
    slots = jnp.arange(capacity, dtype=jnp.int32).astype(F32)[None, :, None]
    taken = jnp.logical_and(hits[:, None, :], ranks[:, None, :] == slots)
    dispatch = taken.astype(BF16).reshape(experts_all * capacity, tok_rows)
    spread = jnp.where(taken, weights[:, None, :], 0.0).reshape(experts_all * capacity, tok_rows)
    high = spread.astype(BF16)
    low = (spread - high.astype(F32)).astype(BF16)
    outgoing = jnp.dot(dispatch, expert_input, preferred_element_type=F32).astype(BF16)
    outgoing = outgoing.reshape(experts_all, capacity, expert_input.shape[1])
    arrived = lax.all_to_all(outgoing, "tensor", split_axis=0, concat_axis=0, tiled=True)
    rows_flat = arrived.reshape(-1, arrived.shape[-1])
    gate_out = jnp.dot(rows_flat, w_gate[0], preferred_element_type=F32)
    up_out = jnp.dot(rows_flat, w_up[0], preferred_element_type=F32)
    hidden = (jnp.maximum(gate_out, 0.0) * up_out).astype(BF16)
    produced = jnp.dot(hidden, w_down[0], preferred_element_type=F32).astype(BF16)
    returned = lax.all_to_all(
        produced.reshape(arrived.shape), "tensor", split_axis=0, concat_axis=0, tiled=True
    ).reshape(rows_flat.shape)
    tn = (((0,), (0,)), ((), ()))
    routed_sum = lax.dot_general(
        high, returned, tn, preferred_element_type=F32
    ) + lax.dot_general(low, returned, tn, preferred_element_type=F32)
    mixed = (residual.astype(F32) + routed_sum).astype(BF16)
    return (mixed, cache_pages)


def solution(mesh):
    return jax.shard_map(
        body,
        mesh=mesh,
        in_specs=(
            P(("seq", "tensor"), None),
            P(("seq", "tensor")),
            P("seq", None),
            P(),
            P(None, "tensor"),
            P(None, "tensor"),
            P(),
            P(("seq", "tensor"), None),
            P(("seq", "tensor"), None),
            P("tensor", None, None),
            P("tensor", None, None),
            P("tensor", None, None),
        ),
        out_specs=(P(("seq", "tensor"), None), P(("seq", "tensor"), None, None)),
        check_vma=False,
    )
```

```python
import functools
import math

import jax
import jax.numpy as jnp
from jax import lax
from jax.experimental import pallas as pl
from jax.experimental.pallas import tpu as pltpu
from jax.sharding import PartitionSpec as P

HEADS = 12
KV_HEADS = 2
HEAD = 128
TOP = 4
PAGE = 16
SEGS = 32
CHUNKS = 32
TOK = 128
STEP = 3
NEG = -1e30

epsilon = 1e-06
F32 = jnp.float32
BF16 = jnp.bfloat16


def rms_scaled(values, scales):
    wide = values.astype(F32)
    mean_sq = jnp.mean(wide * wide, axis=-1, keepdims=True)
    return (wide * lax.rsqrt(mean_sq + epsilon) * scales).astype(BF16)


RING = 4
FULL_A, HALF_A, FULL_B, HALF_B, PAIR = 0, 2, 4, 12, 20
COPIES = 36
ORDER = (0, -1, 1, 2)
MESH = pl.DeviceIdType.MESH


class Rings:
    def __init__(self, shards, outs, splits, send, recv, here, rows=(), columns=False):
        self.rows, self.columns = rows, columns
        self.shards, self.outs, self.splits = shards, outs, splits
        self.send, self.recv, self.here = send, recv, here
        self.place = lax.axis_index("tensor")
        self.core = lax.rem(self.place, 2)
        self.px = lax.rem(self.place // 2, RING)
        self.py = self.place // (2 * RING)
        self.started = []
        self.every = range(len(shards))

    def at(self, a, b, flip=0):
        core = self.core
        x = lax.rem(self.px + a * (1 - core) + b * core + RING, RING)
        y = lax.rem(self.py + a * core + b * (1 - core) + RING, RING)
        return (y * RING + x) * 2 + ((1 - core) if flip else core)

    def row(self, a):
        return lax.rem(self.px * (1 - self.core) + self.py * self.core + a + RING, RING)

    def greet(self, barrier):
        for where in ((1, 0), (-1, 0), (0, 1), (0, -1), (0, 0, 1)):
            pl.semaphore_signal(
                barrier, inc=1, device_id={"tensor": self.at(*where)}, device_id_type=MESH
            )
        return 5

    def view(self, n, a, b, part):
        ref = self.outs[n].at[self.row(a) if n in self.rows else self.at(a, b)]
        if part is None:
            return ref
        axis, cut = self.splits[n]
        whole = self.outs[n].shape[1 + axis]
        span = pl.ds(0, cut) if part == 0 else pl.ds(cut, whole - cut)
        return ref.at[span, :] if axis == 0 else ref.at[:, span]

    def copy(self, n, kind, a, b, part, where):
        if self.columns and b == 0:
            src = self.shards[n].at[self.row(a)]
        else:
            src = self.shards[n] if (a == 0 and b == 0) else self.view(n, a, b, part)
        return pltpu.make_async_remote_copy(
            src_ref=src,
            dst_ref=self.view(n, a, b, part),
            send_sem=self.send.at[n, kind],
            recv_sem=self.recv.at[n, kind],
            device_id={"tensor": self.at(*where)},
            device_id_type=MESH,
        )

    def go(self, *what):
        self.copy(*what).start()
        self.started.append(what)

    def landed(self, n, kind, a, b, part):
        self.copy(n, kind, a, b, part, (0, 0, 1)).wait_recv()

    def spread(self, n, k):
        if n in self.rows:
            return
        r = ORDER[k]
        self.go(n, FULL_B + 2 * k, r, 0, None, (0, 1))
        self.go(n, FULL_B + 2 * k + 1, r, 0, None, (0, -1))
        self.go(n, PAIR + k, r, 0, None, (0, 0, 1))

    def own(self, n):
        if self.columns:
            return [
                pltpu.make_async_copy(
                    self.shards[n].at[self.row(r)], self.outs[n].at[self.at(r, 0)], self.here.at[k]
                )
                for k, r in enumerate(ORDER)
            ]
        slot = self.row(0) if n in self.rows else self.place
        return [pltpu.make_async_copy(self.shards[n], self.outs[n].at[slot], self.here.at[n])]

    def begin(self):
        for n in self.every:
            if self.columns:
                for k in range(RING):
                    self.spread(n, k)
            else:
                self.go(n, FULL_A, 0, 0, None, (1, 0))
                self.go(n, FULL_A + 1, 0, 0, None, (-1, 0))
                self.spread(n, 0)
        for n in self.every:
            for c in self.own(n):
                c.start()

    def first_ring(self):
        for n in self.every:
            self.landed(n, FULL_A, -1, 0, None)
            self.go(n, HALF_A, -1, 0, 0, (1, 0))
            self.spread(n, 1)
            self.landed(n, FULL_A + 1, 1, 0, None)
            self.go(n, HALF_A + 1, 1, 0, 1, (-1, 0))
            self.spread(n, 2)

    def second_ring(self, k):
        r = ORDER[k]
        for n in self.every:
            if k == 1 and not self.columns:
                self.landed(n, HALF_A, 2, 0, 0)
                self.landed(n, HALF_A + 1, 2, 0, 1)
                self.spread(n, 3)
            if n in self.rows:
                continue
            self.landed(n, FULL_B + 2 * k, r, -1, None)
            self.go(n, HALF_B + 2 * k, r, -1, 0, (0, 1))
            self.go(n, PAIR + 4 + k, r, -1, None, (0, 0, 1))
            self.landed(n, FULL_B + 2 * k + 1, r, 1, None)
            self.go(n, HALF_B + 2 * k + 1, r, 1, 1, (0, -1))
            self.go(n, PAIR + 8 + k, r, 1, None, (0, 0, 1))

    def last(self):
        for n in self.every:
            for k in range(0 if n in self.rows else RING):
                self.landed(n, HALF_B + 2 * k, ORDER[k], 2, 0)
                self.landed(n, HALF_B + 2 * k + 1, ORDER[k], 2, 1)
                self.go(n, PAIR + 12 + k, ORDER[k], 2, None, (0, 0, 1))

    def finish(self):
        for n in self.every:
            for c in self.own(n):
                c.wait()
            for k in range(0 if n in self.rows else 4 * RING):
                self.landed(n, PAIR + k, 1, 1, None)
        for what in self.started:
            self.copy(*what).wait_send()


def ring_scratch(count):
    return [
        pltpu.SemaphoreType.DMA((count, COPIES)),
        pltpu.SemaphoreType.DMA((count, COPIES)),
        pltpu.SemaphoreType.DMA((max(count, RING),)),
    ]


def gather_kernel(splits, extra, rows, *refs):
    count = len(splits)
    shards, refs = refs[:count], refs[count:]
    sent, refs = refs[:extra], refs[extra:]
    outs, refs = refs[:count], refs[count:]
    got, refs = refs[:extra], refs[extra:]
    rings = Rings(shards, outs, splits, *refs[:3], rows=rows)
    barrier = pltpu.get_barrier_semaphore()
    greeted = rings.greet(barrier)
    steps = []
    if extra:
        seq = lax.axis_index("seq")
        seq_size = lax.axis_size("seq")
        later = lax.rem(seq + 1, seq_size)
        for peer in (later, lax.rem(seq + seq_size - 1, seq_size)):
            pl.semaphore_signal(barrier, inc=1, device_id={"seq": peer}, device_id_type=MESH)
        greeted += 2
    pl.semaphore_wait(barrier, greeted)
    rings.begin()
    for i in range(extra):
        z = pltpu.make_async_remote_copy(
            src_ref=sent[i],
            dst_ref=got[i],
            send_sem=refs[3].at[2 * i],
            recv_sem=refs[3].at[2 * i + 1],
            device_id={"seq": later},
            device_id_type=MESH,
        )
        z.start()
        steps.append(z)
    rings.first_ring()
    for k in range(RING):
        rings.second_ring(k)
    rings.last()
    for z in steps:
        z.wait()
    rings.finish()


def gather(shards, splits, number, sent=(), rows=()):
    places = lax.axis_size("tensor")
    vm = pl.BlockSpec(memory_space=pltpu.VMEM)
    anyspace = pl.BlockSpec(memory_space=pl.ANY)
    return pl.pallas_call(
        functools.partial(gather_kernel, splits, len(sent), rows),
        out_shape=[
            jax.ShapeDtypeStruct((RING if n in rows else places,) + s.shape, s.dtype)
            for n, s in enumerate(shards)
        ]
        + [jax.ShapeDtypeStruct(s.shape, s.dtype) for s in sent],
        in_specs=[vm] * (len(shards) + len(sent)),
        out_specs=[anyspace] * len(shards) + [vm] * len(sent),
        scratch_shapes=ring_scratch(len(shards))
        + ([pltpu.SemaphoreType.DMA((2 * len(sent),))] if sent else []),
        compiler_params=pltpu.CompilerParams(collective_id=number, has_side_effects=True),
        name="gather_%d" % number,
    )(*shards, *sent)


def attention_kernel(
    starts_ref, q_ref, w_ref, kv_ref, out_ref, gathered_ref, kv, top, total, acc, chunk_sem, *sems
):
    place = lax.axis_index("tensor")
    rings = Rings([w_ref], [gathered_ref], [(1, w_ref.shape[2] // 2)], *sems, columns=True)
    barrier = pltpu.get_barrier_semaphore()
    greeted = rings.greet(barrier)

    def fetch(i):
        w = place + i
        block = w // CHUNKS
        row = pl.multiple_of((1 - block) * TOK, TOK)
        return pltpu.make_async_copy(
            kv_ref.at[w - block * CHUNKS, pl.ds(row, TOK), :], kv.at[i], chunk_sem.at[i]
        )

    def fetch_step(i, _):
        fetch(i).start()
        return 0

    lax.fori_loop(0, CHUNKS + 1, fetch_step, 0)
    scale = math.log2(math.e) / math.sqrt(HEAD)
    group_heads = HEADS // KV_HEADS
    top[...] = jnp.full_like(top, NEG)
    total[...] = jnp.zeros_like(total)
    acc[...] = jnp.zeros_like(acc)
    pl.semaphore_wait(barrier, greeted)
    rings.begin()
    starts = starts_ref[...]
    query = lax.broadcasted_iota(jnp.int32, (STEP * TOK, TOK), 1) + CHUNKS * TOK
    local = lax.broadcasted_iota(jnp.int32, (STEP * TOK, TOK), 0)

    def step(number, _):
        first = number * STEP
        for k in range(RING):
            pl.when(number == 2 + k)(functools.partial(rings.second_ring, k))
        pl.when(number == 9)(rings.last)
        for i in range(STEP):
            fetch(first + i).wait()
        pieces = [kv.at[first + i] for i in range(STEP)]
        pos = local + first * TOK
        allowed = (pos >= starts) & (pos <= query)
        for g in range(KV_HEADS):
            keys = jnp.concatenate([p[:, g * HEAD : (g + 1) * HEAD] for p in pieces], axis=0)
            vals = jnp.concatenate(
                [p[:, (KV_HEADS + g) * HEAD : (KV_HEADS + g + 1) * HEAD] for p in pieces], axis=0
            )
            for h in range(group_heads):
                head = g * group_heads + h
                s = lax.dot_general(
                    keys,
                    q_ref[:, head * HEAD : (head + 1) * HEAD],
                    (((1,), (1,)), ((), ())),
                    preferred_element_type=F32,
                )
                s = jnp.where(allowed, s * scale, NEG)
                old = top[head : head + 1, :]
                new = jnp.maximum(old, jnp.max(s, axis=0, keepdims=True))
                alpha = jnp.exp2(old - new)
                w = jnp.exp2(s - new)
                top[head : head + 1, :] = new
                total[head : head + 1, :] = total[head : head + 1, :] * alpha + jnp.sum(
                    w, axis=0, keepdims=True
                )
                got = lax.dot_general(
                    vals, w.astype(BF16), (((0,), (0,)), ((), ())), preferred_element_type=F32
                )
                acc[head] = acc[head] * alpha + got
        return 0

    lax.fori_loop(0, (CHUNKS + 1) // STEP, step, 0)
    for head in range(HEADS):
        out_ref[head] = (acc[head] / total[head : head + 1, :]).astype(BF16)
    rings.finish()


def attention(starts, q, w_rows, kv_all):
    vm = pl.BlockSpec(memory_space=pltpu.VMEM)
    anyspace = pl.BlockSpec(memory_space=pl.ANY)
    return pl.pallas_call(
        attention_kernel,
        out_shape=[
            jax.ShapeDtypeStruct((HEADS, HEAD, TOK), BF16),
            jax.ShapeDtypeStruct((CHUNKS,) + w_rows.shape[1:], BF16),
        ],
        in_specs=[vm, vm, vm, anyspace],
        out_specs=[vm, anyspace],
        scratch_shapes=[
            pltpu.VMEM((CHUNKS + 1, TOK, kv_all.shape[2]), BF16),
            pltpu.VMEM((16, TOK), F32),
            pltpu.VMEM((16, TOK), F32),
            pltpu.VMEM((HEADS, HEAD, TOK), F32),
            pltpu.SemaphoreType.DMA((CHUNKS + 1,)),
        ]
        + ring_scratch(1),
        compiler_params=pltpu.CompilerParams(collective_id=2, has_side_effects=True),
        name="window_attention",
    )(starts, q, w_rows, kv_all)


def body(
    tokens,
    segment_ids,
    page_table,
    attn_gain,
    w_qkv,
    w_out,
    moe_gain,
    route_ids,
    route_weight,
    w_gate,
    w_up,
    w_down,
):
    tok_rows = tokens.shape[0]
    tensor_size = lax.axis_size("tensor")
    tensor_index = lax.axis_index("tensor")
    seq_index = lax.axis_index("seq")
    query_width = HEADS * HEAD

    counts = jnp.sum(
        (segment_ids[:, None] < jnp.arange(TOK, dtype=jnp.int32)[None, :]).astype(F32), axis=0
    ).astype(BF16)
    count_rows = jnp.broadcast_to(counts[None, :], (PAGE, TOK))
    qkv_t, earlier, earlier_counts = gather(
        [w_qkv.T], [(0, w_qkv.shape[1] // 2)], 0, (tokens, count_rows)
    )
    qkv_t = qkv_t.reshape(-1, tokens.shape[1])
    normed = rms_scaled(jnp.concatenate([tokens, earlier], axis=0), attn_gain)
    nt = (((1,), (1,)), ((), ()))
    projected = lax.dot_general(normed, qkv_t, nt, preferred_element_type=F32).astype(BF16)
    kv = projected[:, query_width:]
    kvw = kv.shape[1]
    upper = jnp.arange(2 * PAGE)[:, None] < PAGE
    both_counts = jnp.where(
        upper, jnp.tile(count_rows, (2, 1)), jnp.tile(earlier_counts, (2, 1))
    )
    kv_all, counts_all, w_rows = gather(
        [kv, both_counts, w_out.T],
        [(0, tok_rows), (0, PAGE), (1, query_width // 2)],
        1,
        rows=(2,),
    )

    own_counts = counts_all[:, 0, :].astype(F32)
    prev_counts = counts_all[:, PAGE, :].astype(F32)
    order = jnp.arange(tensor_size)[:, None]
    before = jnp.where(seq_index == 0, jnp.full_like(prev_counts, TOK), prev_counts)
    starts_of = jnp.sum(
        jnp.where(order <= tensor_index, own_counts, 0.0)
        + jnp.where(order >= tensor_index, before, 0.0),
        axis=0,
    ).astype(jnp.int32)
    starts = jnp.sum(
        jnp.where(
            segment_ids[None, :] == jnp.arange(TOK, dtype=jnp.int32)[:, None], starts_of[:, None], 0
        ),
        axis=0,
    )
    ctx, out_t = attention(
        starts[None, :], projected[:tok_rows, :query_width], w_rows, kv_all
    )
    out_t = out_t.reshape(-1, query_width)

    pages_here = tok_rows // PAGE
    pages_block = page_table.shape[1]
    slot_ids = tensor_index * pages_here + jnp.arange(pages_here, dtype=jnp.int32)
    matches = page_table[0][None, :] == slot_ids[:, None]
    logical = jnp.sum(
        jnp.where(matches, jnp.arange(pages_block, dtype=jnp.int32)[None, :], 0), axis=1
    )
    cache_pages = jnp.stack(
        [
            lax.dynamic_slice(
                kv_all,
                (logical[i] // pages_here, (logical[i] % pages_here) * PAGE, 0),
                (1, PAGE, kvw),
            )[0]
            for i in range(pages_here)
        ]
    )

    attn_out = lax.dot_general(
        ctx.reshape(query_width, tok_rows), out_t, (((0,), (1,)), ((), ())),
        preferred_element_type=F32,
    )
    residual = (tokens.astype(F32) + attn_out).astype(BF16)
    expert_input = rms_scaled(residual, moe_gain)

    experts_all = w_gate.shape[0] * tensor_size
    capacity = max(2, 3 * tok_rows * TOP // (2 * experts_all))
    picks = route_ids.T[None] == jnp.arange(experts_all, dtype=jnp.int32)[:, None, None]
    hits = jnp.any(picks, axis=1)
    weights = jnp.sum(jnp.where(picks, route_weight.T[None], 0.0), axis=1)
    order_of = jnp.arange(tok_rows, dtype=jnp.int32)
    ahead = (order_of[:, None] < order_of[None, :]).astype(BF16)
    ranks = jnp.dot(hits.astype(BF16), ahead, preferred_element_type=F32)
    slots = jnp.arange(capacity, dtype=jnp.int32).astype(F32)[None, :, None]
    taken = jnp.logical_and(hits[:, None, :], ranks[:, None, :] == slots)
    dispatch = taken.astype(BF16).reshape(experts_all * capacity, tok_rows)
    spread = jnp.where(taken, weights[:, None, :], 0.0).reshape(experts_all * capacity, tok_rows)
    high = spread.astype(BF16)
    low = (spread - high.astype(F32)).astype(BF16)
    outgoing = jnp.dot(dispatch, expert_input, preferred_element_type=F32).astype(BF16)
    outgoing = outgoing.reshape(experts_all, capacity, expert_input.shape[1])
    arrived = lax.all_to_all(outgoing, "tensor", split_axis=0, concat_axis=0, tiled=True)
    rows_flat = arrived.reshape(-1, arrived.shape[-1])
    gate_out = jnp.dot(rows_flat, w_gate[0], preferred_element_type=F32)
    up_out = jnp.dot(rows_flat, w_up[0], preferred_element_type=F32)
    hidden = (jnp.maximum(gate_out, 0.0) * up_out).astype(BF16)
    produced = jnp.dot(hidden, w_down[0], preferred_element_type=F32).astype(BF16)
    returned = lax.all_to_all(
        produced.reshape(arrived.shape), "tensor", split_axis=0, concat_axis=0, tiled=True
    ).reshape(rows_flat.shape)
    tn = (((0,), (0,)), ((), ()))
    routed_sum = lax.dot_general(
        high, returned, tn, preferred_element_type=F32
    ) + lax.dot_general(low, returned, tn, preferred_element_type=F32)
    mixed = (residual.astype(F32) + routed_sum).astype(BF16)
    return (mixed, cache_pages)


def solution(mesh):
    return jax.shard_map(
        body,
        mesh=mesh,
        in_specs=(
            P(("seq", "tensor"), None),
            P(("seq", "tensor")),
            P("seq", None),
            P(),
            P(None, "tensor"),
            P(None, "tensor"),
            P(),
            P(("seq", "tensor"), None),
            P(("seq", "tensor"), None),
            P("tensor", None, None),
            P("tensor", None, None),
            P("tensor", None, None),
        ),
        out_specs=(P(("seq", "tensor"), None), P(("seq", "tensor"), None, None)),
        check_vma=False,
    )
```

```python
import functools
import math

import jax
import jax.numpy as jnp
from jax import lax
from jax.experimental import pallas as pl
from jax.experimental.pallas import tpu as pltpu
from jax.sharding import PartitionSpec as P

HEADS = 12
KV_HEADS = 2
HEAD = 128
TOP = 4
PAGE = 16
SEGS = 32
CHUNKS = 32
TOK = 128
STEP = 3
NEG = -1e30

epsilon = 1e-06
F32 = jnp.float32
BF16 = jnp.bfloat16


def rms_scaled(values, scales):
    wide = values.astype(F32)
    mean_sq = jnp.mean(wide * wide, axis=-1, keepdims=True)
    return (wide * lax.rsqrt(mean_sq + epsilon) * scales).astype(BF16)


RING = 4
FULL_A, HALF_A, FULL_B, HALF_B, PAIR = 0, 2, 4, 12, 20
COPIES = 36
ORDER = (0, -1, 1, 2)
MESH = pl.DeviceIdType.MESH


class Rings:
    def __init__(self, shards, outs, splits, send, recv, here, rows=(), columns=False):
        self.rows, self.columns = rows, columns
        self.shards, self.outs, self.splits = shards, outs, splits
        self.send, self.recv, self.here = send, recv, here
        self.place = lax.axis_index("tensor")
        self.core = lax.rem(self.place, 2)
        self.px = lax.rem(self.place // 2, RING)
        self.py = self.place // (2 * RING)
        self.started = []
        self.every = range(len(shards))

    def at(self, a, b, flip=0):
        core = self.core
        x = lax.rem(self.px + a * (1 - core) + b * core + RING, RING)
        y = lax.rem(self.py + a * core + b * (1 - core) + RING, RING)
        return (y * RING + x) * 2 + ((1 - core) if flip else core)

    def row(self, a):
        return lax.rem(self.px * (1 - self.core) + self.py * self.core + a + RING, RING)

    def greet(self, barrier):
        for where in ((1, 0), (-1, 0), (0, 1), (0, -1), (0, 0, 1)):
            pl.semaphore_signal(
                barrier, inc=1, device_id={"tensor": self.at(*where)}, device_id_type=MESH
            )
        return 5

    def view(self, n, a, b, part):
        ref = self.outs[n].at[self.row(a) if n in self.rows else self.at(a, b)]
        if part is None:
            return ref
        axis, cut = self.splits[n]
        whole = self.outs[n].shape[1 + axis]
        span = pl.ds(0, cut) if part == 0 else pl.ds(cut, whole - cut)
        return ref.at[span, :] if axis == 0 else ref.at[:, span]

    def copy(self, n, kind, a, b, part, where):
        if self.columns and b == 0:
            src = self.shards[n].at[self.row(a)]
        else:
            src = self.shards[n] if (a == 0 and b == 0) else self.view(n, a, b, part)
        return pltpu.make_async_remote_copy(
            src_ref=src,
            dst_ref=self.view(n, a, b, part),
            send_sem=self.send.at[n, kind],
            recv_sem=self.recv.at[n, kind],
            device_id={"tensor": self.at(*where)},
            device_id_type=MESH,
        )

    def go(self, *what):
        self.copy(*what).start()
        self.started.append(what)

    def landed(self, n, kind, a, b, part):
        self.copy(n, kind, a, b, part, (0, 0, 1)).wait_recv()

    def spread(self, n, k):
        if n in self.rows:
            return
        r = ORDER[k]
        self.go(n, FULL_B + 2 * k, r, 0, None, (0, 1))
        self.go(n, FULL_B + 2 * k + 1, r, 0, None, (0, -1))
        self.go(n, PAIR + k, r, 0, None, (0, 0, 1))

    def own(self, n):
        if self.columns:
            return [
                pltpu.make_async_copy(
                    self.shards[n].at[self.row(r)], self.outs[n].at[self.at(r, 0)], self.here.at[k]
                )
                for k, r in enumerate(ORDER)
            ]
        slot = self.row(0) if n in self.rows else self.place
        return [pltpu.make_async_copy(self.shards[n], self.outs[n].at[slot], self.here.at[n])]

    def begin(self):
        for n in self.every:
            if self.columns:
                for k in range(RING):
                    self.spread(n, k)
            else:
                self.go(n, FULL_A, 0, 0, None, (1, 0))
                self.go(n, FULL_A + 1, 0, 0, None, (-1, 0))
                self.spread(n, 0)
        for n in self.every:
            for c in self.own(n):
                c.start()

    def first_ring(self):
        for n in self.every:
            self.landed(n, FULL_A, -1, 0, None)
            self.go(n, HALF_A, -1, 0, 0, (1, 0))
            self.spread(n, 1)
            self.landed(n, FULL_A + 1, 1, 0, None)
            self.go(n, HALF_A + 1, 1, 0, 1, (-1, 0))
            self.spread(n, 2)

    def second_ring(self, k):
        r = ORDER[k]
        for n in self.every:
            if k == 1 and not self.columns:
                self.landed(n, HALF_A, 2, 0, 0)
                self.landed(n, HALF_A + 1, 2, 0, 1)
                self.spread(n, 3)
            if n in self.rows:
                continue
            self.landed(n, FULL_B + 2 * k, r, -1, None)
            self.go(n, HALF_B + 2 * k, r, -1, 0, (0, 1))
            self.go(n, PAIR + 4 + k, r, -1, None, (0, 0, 1))
            self.landed(n, FULL_B + 2 * k + 1, r, 1, None)
            self.go(n, HALF_B + 2 * k + 1, r, 1, 1, (0, -1))
            self.go(n, PAIR + 8 + k, r, 1, None, (0, 0, 1))

    def last(self):
        for n in self.every:
            for k in range(0 if n in self.rows else RING):
                self.landed(n, HALF_B + 2 * k, ORDER[k], 2, 0)
                self.landed(n, HALF_B + 2 * k + 1, ORDER[k], 2, 1)
                self.go(n, PAIR + 12 + k, ORDER[k], 2, None, (0, 0, 1))

    def finish(self):
        for n in self.every:
            for c in self.own(n):
                c.wait()
            for k in range(0 if n in self.rows else 4 * RING):
                self.landed(n, PAIR + k, 1, 1, None)
        for what in self.started:
            self.copy(*what).wait_send()


def ring_scratch(count):
    return [
        pltpu.SemaphoreType.DMA((count, COPIES)),
        pltpu.SemaphoreType.DMA((count, COPIES)),
        pltpu.SemaphoreType.DMA((max(count, RING),)),
    ]


def gather_kernel(splits, extra, rows, *refs):
    count = len(splits)
    shards, refs = refs[:count], refs[count:]
    sent, refs = refs[:extra], refs[extra:]
    outs, refs = refs[:count], refs[count:]
    got, refs = refs[:extra], refs[extra:]
    shards = [
        s.at[:, pl.ds(s.shape[1] - o.shape[-1], o.shape[-1])] if s.shape[1] > o.shape[-1] else s
        for s, o in zip(shards, outs)
    ]
    rings = Rings(shards, outs, splits, *refs[:3], rows=rows)
    barrier = pltpu.get_barrier_semaphore()
    greeted = rings.greet(barrier)
    steps = []
    if extra:
        seq = lax.axis_index("seq")
        seq_size = lax.axis_size("seq")
        later = lax.rem(seq + 1, seq_size)
        for peer in (later, lax.rem(seq + seq_size - 1, seq_size)):
            pl.semaphore_signal(barrier, inc=1, device_id={"seq": peer}, device_id_type=MESH)
        greeted += 2
    pl.semaphore_wait(barrier, greeted)
    rings.begin()
    for i in range(extra):
        z = pltpu.make_async_remote_copy(
            src_ref=sent[i],
            dst_ref=got[i],
            send_sem=refs[3].at[2 * i],
            recv_sem=refs[3].at[2 * i + 1],
            device_id={"seq": later},
            device_id_type=MESH,
        )
        z.start()
        steps.append(z)
    rings.first_ring()
    for k in range(RING):
        rings.second_ring(k)
    rings.last()
    for z in steps:
        z.wait()
    rings.finish()


def gather(shards, splits, number, sent=(), rows=(), widths=None):
    places = lax.axis_size("tensor")
    vm = pl.BlockSpec(memory_space=pltpu.VMEM)
    anyspace = pl.BlockSpec(memory_space=pl.ANY)
    return pl.pallas_call(
        functools.partial(gather_kernel, splits, len(sent), rows),
        out_shape=[
            jax.ShapeDtypeStruct(
                (RING if n in rows else places, s.shape[0], widths[n] if widths else s.shape[1]),
                s.dtype,
            )
            for n, s in enumerate(shards)
        ]
        + [jax.ShapeDtypeStruct(s.shape, s.dtype) for s in sent],
        in_specs=[vm] * (len(shards) + len(sent)),
        out_specs=[anyspace] * len(shards) + [vm] * len(sent),
        scratch_shapes=ring_scratch(len(shards))
        + ([pltpu.SemaphoreType.DMA((2 * len(sent),))] if sent else []),
        compiler_params=pltpu.CompilerParams(collective_id=number, has_side_effects=True),
        name="gather_%d" % number,
    )(*shards, *sent)


def attention_kernel(
    starts_ref, q_ref, w_ref, kv_ref, out_ref, gathered_ref, kv, top, total, acc, chunk_sem, *sems
):
    place = lax.axis_index("tensor")
    rings = Rings([w_ref], [gathered_ref], [(1, w_ref.shape[2] // 2)], *sems, columns=True)
    barrier = pltpu.get_barrier_semaphore()
    greeted = rings.greet(barrier)

    def fetch(i):
        w = place + i
        block = w // CHUNKS
        row = pl.multiple_of((1 - block) * TOK, TOK)
        return pltpu.make_async_copy(
            kv_ref.at[w - block * CHUNKS, pl.ds(row, TOK), :], kv.at[i], chunk_sem.at[i]
        )

    def fetch_step(i, _):
        fetch(i).start()
        return 0

    lax.fori_loop(0, CHUNKS + 1, fetch_step, 0)
    scale = math.log2(math.e) / math.sqrt(HEAD)
    group_heads = HEADS // KV_HEADS
    top[...] = jnp.full_like(top, NEG)
    total[...] = jnp.zeros_like(total)
    acc[...] = jnp.zeros_like(acc)
    pl.semaphore_wait(barrier, greeted)
    rings.begin()
    starts = starts_ref[...]
    query = lax.broadcasted_iota(jnp.int32, (STEP * TOK, TOK), 1) + CHUNKS * TOK
    local = lax.broadcasted_iota(jnp.int32, (STEP * TOK, TOK), 0)

    def step(number, _):
        first = number * STEP
        for k in range(RING):
            pl.when(number == 2 + k)(functools.partial(rings.second_ring, k))
        pl.when(number == 9)(rings.last)
        for i in range(STEP):
            fetch(first + i).wait()
        pieces = [kv.at[first + i] for i in range(STEP)]
        pos = local + first * TOK
        allowed = (pos >= starts) & (pos <= query)
        for g in range(KV_HEADS):
            keys = jnp.concatenate([p[:, g * HEAD : (g + 1) * HEAD] for p in pieces], axis=0)
            vals = jnp.concatenate(
                [p[:, (KV_HEADS + g) * HEAD : (KV_HEADS + g + 1) * HEAD] for p in pieces], axis=0
            )
            for h in range(group_heads):
                head = g * group_heads + h
                s = lax.dot_general(
                    keys,
                    q_ref[:TOK, head * HEAD : (head + 1) * HEAD],
                    (((1,), (1,)), ((), ())),
                    preferred_element_type=F32,
                )
                s = jnp.where(allowed, s * scale, NEG)
                old = top[head : head + 1, :]
                new = jnp.maximum(old, jnp.max(s, axis=0, keepdims=True))
                alpha = jnp.exp2(old - new)
                w = jnp.exp2(s - new)
                top[head : head + 1, :] = new
                total[head : head + 1, :] = total[head : head + 1, :] * alpha + jnp.sum(
                    w, axis=0, keepdims=True
                )
                got = lax.dot_general(
                    vals, w.astype(BF16), (((0,), (0,)), ((), ())), preferred_element_type=F32
                )
                acc[head] = acc[head] * alpha + got
        return 0

    lax.fori_loop(0, (CHUNKS + 1) // STEP, step, 0)
    for head in range(HEADS):
        out_ref[head] = (acc[head] / total[head : head + 1, :]).astype(BF16)
    rings.finish()


def attention(starts, q, w_rows, kv_all):
    vm = pl.BlockSpec(memory_space=pltpu.VMEM)
    anyspace = pl.BlockSpec(memory_space=pl.ANY)
    return pl.pallas_call(
        attention_kernel,
        out_shape=[
            jax.ShapeDtypeStruct((HEADS, HEAD, TOK), BF16),
            jax.ShapeDtypeStruct((CHUNKS,) + w_rows.shape[1:], BF16),
        ],
        in_specs=[vm, vm, vm, anyspace],
        out_specs=[vm, anyspace],
        scratch_shapes=[
            pltpu.VMEM((CHUNKS + 1, TOK, kv_all.shape[2]), BF16),
            pltpu.VMEM((16, TOK), F32),
            pltpu.VMEM((16, TOK), F32),
            pltpu.VMEM((HEADS, HEAD, TOK), F32),
            pltpu.SemaphoreType.DMA((CHUNKS + 1,)),
        ]
        + ring_scratch(1),
        compiler_params=pltpu.CompilerParams(collective_id=2, has_side_effects=True),
        name="window_attention",
    )(starts, q, w_rows, kv_all)


def body(
    tokens,
    segment_ids,
    page_table,
    attn_gain,
    w_qkv,
    w_out,
    moe_gain,
    route_ids,
    route_weight,
    w_gate,
    w_up,
    w_down,
):
    tok_rows = tokens.shape[0]
    tensor_size = lax.axis_size("tensor")
    tensor_index = lax.axis_index("tensor")
    seq_index = lax.axis_index("seq")
    query_width = HEADS * HEAD

    counts = jnp.sum(
        (segment_ids[:, None] < jnp.arange(TOK, dtype=jnp.int32)[None, :]).astype(F32), axis=0
    ).astype(BF16)
    count_rows = jnp.broadcast_to(counts[None, :], (PAGE, TOK))
    qkv_t, earlier, earlier_counts = gather(
        [w_qkv.T], [(0, w_qkv.shape[1] // 2)], 0, (tokens, count_rows)
    )
    qkv_t = qkv_t.reshape(-1, tokens.shape[1])
    normed = rms_scaled(jnp.concatenate([tokens, earlier], axis=0), attn_gain)
    nt = (((1,), (1,)), ((), ()))
    projected = lax.dot_general(normed, qkv_t, nt, preferred_element_type=F32).astype(BF16)
    kvw = projected.shape[1] - query_width
    upper = jnp.arange(2 * PAGE)[:, None] < PAGE
    both_counts = jnp.where(
        upper, jnp.tile(count_rows, (2, 1)), jnp.tile(earlier_counts, (2, 1))
    )
    kv_all, counts_all, w_rows = gather(
        [projected, both_counts, w_out.T],
        [(0, tok_rows), (0, PAGE), (1, query_width // 2)],
        1,
        rows=(2,),
        widths=(kvw, TOK, query_width),
    )

    order = jnp.arange(tensor_size)[:, None, None]
    upper_half = jnp.arange(2 * PAGE)[None, :, None] < PAGE
    wide_counts = jnp.where(
        jnp.logical_or(upper_half, seq_index > 0), counts_all.astype(F32), float(TOK)
    )
    wanted = jnp.where(upper_half, order <= tensor_index, order >= tensor_index)
    starts_of = (
        jnp.sum(jnp.where(wanted, wide_counts, 0.0), axis=(0, 1)) * (1.0 / PAGE)
    ).astype(jnp.int32)
    starts = jnp.sum(
        jnp.where(
            segment_ids[None, :] == jnp.arange(TOK, dtype=jnp.int32)[:, None], starts_of[:, None], 0
        ),
        axis=0,
    )
    ctx, out_t = attention(
        starts[None, :], projected, w_rows, kv_all
    )
    out_t = out_t.reshape(-1, query_width)

    pages_here = tok_rows // PAGE
    pages_block = page_table.shape[1]
    slot_ids = tensor_index * pages_here + jnp.arange(pages_here, dtype=jnp.int32)
    matches = page_table[0][None, :] == slot_ids[:, None]
    logical = jnp.sum(
        jnp.where(matches, jnp.arange(pages_block, dtype=jnp.int32)[None, :], 0), axis=1
    )
    cache_pages = jnp.stack(
        [
            lax.dynamic_slice(
                kv_all,
                (logical[i] // pages_here, (logical[i] % pages_here) * PAGE, 0),
                (1, PAGE, kvw),
            )[0]
            for i in range(pages_here)
        ]
    )

    attn_out = lax.dot_general(
        ctx.reshape(query_width, tok_rows), out_t, (((0,), (1,)), ((), ())),
        preferred_element_type=F32,
    )
    residual = (tokens.astype(F32) + attn_out).astype(BF16)
    expert_input = rms_scaled(residual, moe_gain)

    experts_all = w_gate.shape[0] * tensor_size
    capacity = max(2, 3 * tok_rows * TOP // (2 * experts_all))
    picks = route_ids.T[None] == jnp.arange(experts_all, dtype=jnp.int32)[:, None, None]
    hits = jnp.any(picks, axis=1)
    weights = jnp.sum(jnp.where(picks, route_weight.T[None], 0.0), axis=1)
    order_of = jnp.arange(tok_rows, dtype=jnp.int32)
    ahead = (order_of[:, None] < order_of[None, :]).astype(BF16)
    ranks = jnp.dot(hits.astype(BF16), ahead, preferred_element_type=F32)
    slots = jnp.arange(capacity, dtype=jnp.int32).astype(F32)[None, :, None]
    taken = jnp.logical_and(hits[:, None, :], ranks[:, None, :] == slots)
    dispatch = taken.astype(BF16).reshape(experts_all * capacity, tok_rows)
    spread = jnp.where(taken, weights[:, None, :], 0.0).reshape(experts_all * capacity, tok_rows)
    high = spread.astype(BF16)
    low = (spread - high.astype(F32)).astype(BF16)
    outgoing = jnp.dot(dispatch, expert_input, preferred_element_type=F32).astype(BF16)
    outgoing = outgoing.reshape(experts_all, capacity, expert_input.shape[1])
    arrived = lax.all_to_all(outgoing, "tensor", split_axis=0, concat_axis=0, tiled=True)
    rows_flat = arrived.reshape(-1, arrived.shape[-1])
    gate_out = jnp.dot(rows_flat, w_gate[0], preferred_element_type=F32)
    up_out = jnp.dot(rows_flat, w_up[0], preferred_element_type=F32)
    hidden = (jnp.maximum(gate_out, 0.0) * up_out).astype(BF16)
    produced = jnp.dot(hidden, w_down[0], preferred_element_type=F32).astype(BF16)
    returned = lax.all_to_all(
        produced.reshape(arrived.shape), "tensor", split_axis=0, concat_axis=0, tiled=True
    ).reshape(rows_flat.shape)
    tn = (((0,), (0,)), ((), ()))
    both_parts = lax.dot_general(
        jnp.concatenate([high, low], axis=1), returned, tn, preferred_element_type=F32
    )
    routed_sum = both_parts[:tok_rows] + both_parts[tok_rows:]
    mixed = (residual.astype(F32) + routed_sum).astype(BF16)
    return (mixed, cache_pages)


def solution(mesh):
    return jax.shard_map(
        body,
        mesh=mesh,
        in_specs=(
            P(("seq", "tensor"), None),
            P(("seq", "tensor")),
            P("seq", None),
            P(),
            P(None, "tensor"),
            P(None, "tensor"),
            P(),
            P(("seq", "tensor"), None),
            P(("seq", "tensor"), None),
            P("tensor", None, None),
            P("tensor", None, None),
            P("tensor", None, None),
        ),
        out_specs=(P(("seq", "tensor"), None), P(("seq", "tensor"), None, None)),
        check_vma=False,
    )
```
